256 devices in a mesh: segment: 2 (over x_lo), win: 32 (over x_hi, z, core), mp: 4 (over y).
Axes of the slice: x: 4 (x_hi: 2, x_lo: 2; x = x_hi * 2 + x_lo), y: 4, z: 8, core: 2. Of those that a mesh axis runs over, the one named last changes fastest.
Arguments:
- feats: bfloat16 [32, 1536, 256], P('win'), may hold values from -6 to 6
- convolution_kernel_weight: bfloat16 [1536, 5, 1536], P('win', None, 'mp'), may hold values from -0.0625 to 0.0625
- conv_bias: float32 [1536], P('mp'), may hold values from -3 to 3
- qkv_weight: bfloat16 [1536, 2560], P('win', 'mp'), may hold values from -0.15625 to 0.15625
- out_weight: bfloat16 [1536, 1536], P('win', 'mp'), may hold values from -0.15625 to 0.15625
- head_weight: bfloat16 [1536, 4096], P('win', 'mp'), may hold values from -0.15625 to 0.15625
- head_bias: float32 [4096], P('mp'), may hold values from -4 to 4
- exon_lists: int32 [3, 32, 64, 8], P(None, 'win'), may hold values from 0 to 256, as said below
Outputs:
- gene_tracks: float32 [512, 4096], P(('segment', 'win'), 'mp')
The draws below stay inside these ranges and needn't reach their ends.
Inputs may be any that keep to these rules, and one draw needn't show every extreme that they name: `exon_lists`: A slot with equal first and end bin is unused and has gene slot 0; used slots have 1 to 8 bins and a gene slot below 8. In every draw some owners receive 8 used ranges from every window.
All inputs are finite; a program needn't handle non-finite values.
Results may differ from the reference program's by a relative error of at most 0.0025.
Values may be sent and summed in bfloat16 or wider, within the bound.
A program may use at most 64 MiB of HBM per device.

```python
import math
import jax
import jax.numpy as jnp
from jax import lax

D = 1536
HEADS = 8
KEY = 64
VAL = 192
TRACKS = 4096
KERNEL_TAPS = 5
DILATION_STEP = 4
WINDOW_BINS = 256
GENE_DEV = 8
CAP = 8
QKV = 2560
WINDOWS = 32
OWNERS = 64
GENES = 512


def draw_exon_lists(key, part):
    subkeys = jax.random.split(jax.random.fold_in(key, 17), 6)
    heavy_owner = jax.random.randint(subkeys[0], (OWNERS,), 0, 8) == 0
    forced_owner = jax.random.randint(subkeys[1], (), 0, OWNERS)
    heavy_owner = heavy_owner | (jnp.arange(OWNERS) == forced_owner)
    light_counts = jax.random.randint(subkeys[2], (WINDOWS, OWNERS), 0, CAP // 4 + 1)
    counts_all = jnp.where(heavy_owner[None, :], CAP, light_counts)
    is_live = jnp.arange(CAP)[None, None, :] < counts_all[:, :, None]
    range_cap = min(8, WINDOW_BINS)
    draw_shape = (WINDOWS, OWNERS, CAP)
    first_bins = jax.random.randint(subkeys[3], draw_shape, 0, WINDOW_BINS - range_cap + 1)
    lengths_drawn = jax.random.randint(subkeys[4], draw_shape, 1, range_cap + 1)
    gene_slots = jax.random.randint(subkeys[5], draw_shape, 0, GENE_DEV)
    starts = jnp.where(is_live, first_bins, 0)
    end_bins = jnp.where(is_live, first_bins + lengths_drawn, 0)
    gene_slots = jnp.where(is_live, gene_slots, 0)
    return jnp.stack([starts, end_bins, gene_slots]).astype(jnp.int32)


def block_levels(own_key, shape, cuts, least, high):
    loudness = 1.0
    for dim, blocks in cuts:
        draws = jax.random.uniform(jax.random.fold_in(jax.random.fold_in(own_key, 6), dim), (blocks,), jnp.float32, least / len(cuts), high / len(cuts))
        loudness = loudness * jnp.repeat(jnp.exp(draws), shape[dim] // blocks).reshape((-1,) + (1,) * (len(shape) - 1 - dim))
    return loudness


def centred(key, extent, deviation, most, shards=(), held_as=jnp.bfloat16):
    loudness = block_levels(key, extent, shards, -0.22, 0.18) if shards else 1.0
    drawn = jax.random.normal(key, extent, jnp.float32) * deviation * loudness
    return jnp.minimum(jnp.maximum(drawn, -most), most).astype(held_as)


def setup_inputs(seed: int = 0) -> dict:
    arg_keys = jax.random.split(jax.random.key(seed), 9)
    return {
        "feats": centred(arg_keys[0], (WINDOWS, D, WINDOW_BINS), 1.0, 6.0, ((0, 32),)),
        "convolution_kernel_weight": centred(arg_keys[1], (D, KERNEL_TAPS, D), (D * KERNEL_TAPS) ** -0.5, 0.0625, ((0, 32), (2, 4))),
        "conv_bias": centred(arg_keys[2], (D,), 0.5, 3.0, ((0, 4),), jnp.float32),
        "qkv_weight": centred(arg_keys[3], (D, QKV), D ** -0.5, 0.15625, ((0, 32), (1, 4))),
        "out_weight": centred(arg_keys[4], (D, HEADS * VAL), (HEADS * VAL) ** -0.5, 0.15625, ((0, 32), (1, 4))),
        "head_weight": centred(arg_keys[5], (D, TRACKS), D ** -0.5, 0.15625, ((0, 32), (1, 4))),
        "head_bias": centred(arg_keys[6], (TRACKS,), 1.0, 4.0, ((0, 4),), jnp.float32),
        "exon_lists": draw_exon_lists(jax.random.fold_in(arg_keys[8], 71), 0),
    }


def contract_rows(left, right):
    return lax.dot_general(left, right, (((0,), (0,)), ((), ())), preferred_element_type=jnp.float32)

def reference(feats, convolution_kernel_weight, conv_bias, qkv_weight, out_weight, head_weight, head_bias, exon_lists):
    receptive_reach_bins = (KERNEL_TAPS - 1) // 2 * DILATION_STEP
    head_span = 2 * KEY + VAL
    score_scale = 1.0 / math.sqrt(KEY)
    position = jnp.arange(WINDOW_BINS, dtype=jnp.int32)
    gene_ids = jnp.arange(GENES, dtype=jnp.int32)
    owner_base = (jnp.arange(OWNERS, dtype=jnp.int32) * GENE_DEV)[:, None]

    def one_window(gene_total, inputs):
        source, ranges = inputs
        padded_input = jnp.pad(source, ((0, 0), (receptive_reach_bins, receptive_reach_bins)))
        conv_pre = jnp.zeros((D, WINDOW_BINS), jnp.float32)
        for tap_index in range(KERNEL_TAPS):
            shifted_input = padded_input[:, tap_index * DILATION_STEP:tap_index * DILATION_STEP + WINDOW_BINS]
            conv_pre = conv_pre + contract_rows(convolution_kernel_weight[:, tap_index, :], shifted_input)
        conv_out = (source + jax.nn.gelu(conv_pre + conv_bias[:, None])).astype(jnp.bfloat16)
        qkv_rows = contract_rows(qkv_weight, conv_out).astype(jnp.bfloat16)
        outputs = []
        for head_idx in range(HEADS):
            offset = head_idx * head_span
            query_rows = qkv_rows[offset:offset + KEY]
            key_rows = qkv_rows[offset + KEY:offset + 2 * KEY]
            value_rows = qkv_rows[offset + 2 * KEY:offset + head_span]
            scores = contract_rows(query_rows, key_rows) * score_scale
            weights = jnp.exp(scores)
            prob_rows = (weights / lax.optimization_barrier(jnp.sum(weights, axis=1, keepdims=True))).astype(jnp.bfloat16)
            head_out = lax.dot_general(value_rows, prob_rows, (((1,), (1,)), ((), ())), preferred_element_type=jnp.float32)
            outputs.append(head_out.astype(jnp.bfloat16))
        joined = jnp.concatenate(outputs, axis=0)
        attn_out = lax.dot_general(out_weight, joined, (((1,), (0,)), ((), ())), preferred_element_type=jnp.float32)
        resid = (conv_out + attn_out).astype(jnp.bfloat16)
        logits = contract_rows(head_weight, resid) + head_bias[:, None]
        tracks = jax.nn.softplus(logits).astype(jnp.bfloat16)
        starts = ranges[0].reshape(-1)
        end_bins = ranges[1].reshape(-1)
        inside = (position[None, :] >= starts[:, None]) & (position[None, :] < end_bins[:, None])
        entry_sum = lax.dot_general(inside.astype(jnp.bfloat16), tracks, (((1,), (1,)), ((), ())), preferred_element_type=jnp.float32)
        global_ids = (ranges[2] + owner_base).reshape(-1)
        onehot = (global_ids[:, None] == gene_ids[None, :]).astype(jnp.float32)
        gene_total = gene_total + lax.dot_general(onehot, entry_sum, (((0,), (0,)), ((), ())), precision=lax.Precision.HIGHEST, preferred_element_type=jnp.float32)
        return (gene_total, None)
    ranges_all = jnp.moveaxis(exon_lists, 1, 0)
    gene_total, unused = lax.scan(one_window, jnp.zeros((GENES, TRACKS), jnp.float32), (feats, ranges_all))
    return jnp.log1p(gene_total)
```

```python
import math

import jax
import jax.numpy as jnp
from jax import lax
from jax.experimental import pallas as pl
from jax.experimental.pallas import tpu as pltpu
from jax.sharding import PartitionSpec as P

MESH = pl.DeviceIdType.MESH
F32 = jnp.float32
BF16 = jnp.bfloat16

KEY = 64
VAL = 192
TAPS = 5
STEP = 4
BINS = 256
D = 1536
ROWS = 48
COLS = 192
HALF = COLS // 2
P1 = 1024
P2 = 768
TRK = 512
NZ = 8
NY = 4

FORWARD = {
    ("O", 0): ("zp", "zm", "xp", "cp"),
    ("O", -1): ("zp", "cp"),
    ("O", -2): ("zp", "xp", "cp"),
    ("O", -3): ("zp", "xp", "cp"),
    ("O", -4): ("xp", "cp"),
    ("O", 1): ("zm", "cp"),
    ("O", 2): ("zm", "cp"),
    ("O", 3): ("xp", "cp"),
    ("X", 0): ("zp", "zm", "cp"),
    ("X", -1): ("cp",),
    ("X", 1): ("zm", "cp"),
    ("X", 2): ("cp",),
    ("X", -2): ("cp",),
    ("X", -3): ("cp",),
    ("X", 3): ("cp",),
    ("X", -4): ("cp",),
}
ROUNDS = (
    (("O", 0),),
    (("O", -1), ("O", 1), ("X", 0)),
    (("O", -2), ("O", 2), ("X", -1), ("X", 1)),
    (("O", -3), ("O", 3), ("X", -2), ("X", 2)),
    (("O", -4), ("X", -3), ("X", 3)),
    (("X", -4),),
)
SHARDS = tuple(code for group in ROUNDS for code in group)


def nt(left, right):
    return lax.dot_general(left, right, (((1,), (1,)), ((), ())), preferred_element_type=F32)


def nn(left, right):
    return lax.dot_general(left, right, (((1,), (0,)), ((), ())), preferred_element_type=F32)


def tn(left, right):
    return lax.dot_general(left, right, (((0,), (0,)), ((), ())), preferred_element_type=F32)


def gelu(x):
    return 0.5 * x * (1.0 + jnp.tanh(math.sqrt(2.0 / math.pi) * (x + 0.044715 * (x * x * x))))


def kernel(
    feats, p1, p2, outw, cbias, hbias, exon,
    out,
    w1, w2, wo, gx, ga, gr, ft, y, wqt, w2t, trk, gmat, ex_out, ex_in, gs, gin,
    rs1, ss1, rs2, ss2, rsw, ssw, rsy, ssy, rsa, ssa, rsg, ssg, rse, sse, lsem,
):
    s = lax.axis_index("segment")
    w = lax.axis_index("win")
    m = lax.axis_index("mp")
    h = w // (2 * NZ)
    z = (w // 2) % NZ
    c = w % 2
    b = (s + h) % 2
    q = 2 * m + b

    def win_of(hh, zz, cc):
        return hh * (2 * NZ) + zz * 2 + cc

    where = {
        "zp": {"win": win_of(h, (z + 1) % NZ, c)},
        "zm": {"win": win_of(h, (z + NZ - 1) % NZ, c)},
        "xp": {"segment": 1 - s, "win": win_of(1 - h, z, c)},
        "cp": {"win": win_of(h, z, 1 - c)},
        "sp": {"segment": 1 - s},
        "yp": {"mp": (m + 1) % NY},
        "ym": {"mp": (m + NY - 1) % NY},
        "y2": {"mp": (m + 2) % NY},
    }

    def to(name):
        d = {"segment": s, "win": w, "mp": m}
        d.update(where[name])
        return (d["segment"], d["win"], d["mp"])

    barrier = pltpu.get_barrier_semaphore()
    for name in where:
        pl.semaphore_signal(barrier, inc=1, device_id=to(name), device_id_type=MESH)
    pl.semaphore_wait(barrier, len(where))

    def remote(src, dst, send, recv, device):
        return pltpu.make_async_remote_copy(
            src_ref=src, dst_ref=dst, send_sem=send, recv_sem=recv, device_id=device, device_id_type=MESH
        )

    sent = []

    def shard_win(code, core):
        kind, d = code
        return win_of(h if kind == "O" else 1 - h, (z + d + NZ) % NZ, core)

    def ring(own, buf, send, recv):
        count = [0]
        tail = []

        def rows(win):
            return buf.at[pl.ds(pl.multiple_of(win * ROWS, ROWS), ROWS), :]

        def step(r):
            for code in ROUNDS[r]:
                win = shard_win(code, c)
                src = own if code == ("O", 0) else rows(win)
                if code != ("O", 0):
                    remote(src, rows(win), send.at[0], recv.at[win], to("cp")).wait_recv()
                for name in FORWARD[code]:
                    copy = remote(src, rows(win), send.at[count[0]], recv.at[win], to(name))
                    count[0] += 1
                    copy.start()
                    tail.append(copy)

        def rest():
            for code in SHARDS:
                win = shard_win(code, 1 - c)
                remote(rows(win), rows(win), send.at[0], recv.at[win], to("cp")).wait_recv()

        def flush():
            for copy in tail:
                copy.wait_send()

        return step, rest, flush

    def wo_rows(win):
        return wo.at[pl.ds(pl.multiple_of((win % 4) * ROWS, ROWS), ROWS), :]

    def wo_part(win, model):
        return wo.at[
            pl.ds(pl.multiple_of((win % 4) * ROWS, ROWS), ROWS),
            pl.ds(pl.multiple_of(model * 2 * COLS, 2 * COLS), 2 * COLS),
        ]

    home = (w // 4) // 2
    mine = (w // 4) % 2 == b
    wo_hop = (home - m + NY) % NY
    wo_send = jnp.logical_and(mine, wo_hop != 0)
    wo_keep = jnp.logical_and(mine, wo_hop == 0)

    def wo_hop_copy():
        return remote(outw, wo_part(w, m), ssy.at[0], rsy.at[wo_hop], (s, w, home))

    def wo_start():
        @pl.when(wo_send)
        def _():
            wo_hop_copy().start()

        @pl.when(wo_keep)
        def _():
            pltpu.make_async_copy(outw, wo_part(w, m), lsem.at[2]).start()

    wo_count = [0]
    wo_tail = []

    def wo_step(r):
        for code in ROUNDS[r]:
            win = shard_win(code, c)
            first = wo_count[0]
            wo_count[0] += len(FORWARD[code])

            def copies(win=win, code=code, first=first):
                return [
                    remote(wo_rows(win), wo_rows(win), ssw.at[first + i], rsw.at[win % 4], to(name))
                    for i, name in enumerate(FORWARD[code])
                ]

            pred = win // 4 == q
            wo_tail.append((pred, copies))

            @pl.when(pred)
            def _(win=win, code=code, copies=copies):
                if code == ("O", 0):
                    pltpu.make_async_copy(outw, wo_part(w, m), lsem.at[2]).wait()
                    for j in range(1, NY):
                        part = wo_part(w, (m - j + NY) % NY)
                        remote(outw, part, ssy.at[0], rsy.at[j], to("cp")).wait_recv()
                else:
                    remote(wo_rows(win), wo_rows(win), ssw.at[0], rsw.at[win % 4], to("cp")).wait_recv()
                for copy in copies():
                    copy.start()

    def wo_rest():
        for code in SHARDS:
            win = shard_win(code, 1 - c)

            @pl.when(win // 4 == q)
            def _(win=win):
                remote(wo_rows(win), wo_rows(win), ssw.at[0], rsw.at[win % 4], to("cp")).wait_recv()

    def wo_flush():
        @pl.when(wo_send)
        def _():
            wo_hop_copy().wait_send()

        for pred, copies in wo_tail:
            @pl.when(pred)
            def _(copies=copies):
                for copy in copies():
                    copy.wait_send()

    def gather(buf, which):
        def slot(dm, other):
            bb = 1 - b if other else b
            return 2 * ((m + dm + NY) % NY) + bb

        def rows(dm, other, lo=0, n=COLS):
            return buf.at[pl.ds(pl.multiple_of(slot(dm, other) * COLS + lo, 32), n), :]

        def sem(i):
            return rsa.at[which * 9 + i]

        tail = []

        def push(i, r, ref, name):
            copy = remote(ref, ref, ssa.at[which * 9 + i], sem(r), to(name))
            copy.start()
            tail.append(copy)

        def got(r, ref):
            remote(ref, ref, ssa.at[which * 9], sem(r), to("sp")).wait_recv()

        def start():
            own = rows(0, False)
            push(0, 0, own, "yp")
            push(1, 1, own, "ym")
            push(2, 2, own, "sp")

        def first():
            got(0, rows(-1, False))
            push(3, 3, rows(-1, False, 0, HALF), "yp")
            got(1, rows(1, False))
            push(4, 4, rows(1, False, HALF, HALF), "ym")
            got(2, rows(0, True))
            push(5, 5, rows(0, True), "yp")
            push(6, 6, rows(0, True), "ym")

        def second():
            got(3, rows(2, False, 0, HALF))
            got(4, rows(2, False, HALF, HALF))
            push(7, 7, rows(2, False), "sp")

        def third():
            got(5, rows(-1, True))
            got(6, rows(1, True))
            got(7, rows(2, True))

        def flush():
            for copy in tail:
                copy.wait_send()

        return start, first, second, third, flush

    step1, rest1, flush1 = ring(p1, w1, ss1, rs1)
    step2, rest2, flush2 = ring(p2, w2, ss2, rs2)

    step1(0)
    keep1 = pltpu.make_async_copy(p1, w1.at[pl.ds(pl.multiple_of(w * ROWS, ROWS), ROWS), :], lsem.at[0])
    keep2 = pltpu.make_async_copy(p2, w2.at[pl.ds(pl.multiple_of(w * ROWS, ROWS), ROWS), :], lsem.at[1])
    keep1.start()
    keep2.start()
    wo_start()

    eye = (
        lax.broadcasted_iota(jnp.int32, (BINS, BINS), 0) == lax.broadcasted_iota(jnp.int32, (BINS, BINS), 1)
    ).astype(F32).astype(BF16)

    @pl.loop(0, D // BINS)
    def _(n):
        at = pl.ds(pl.multiple_of(n * BINS, BINS), BINS)
        ft[:, at] = nt(eye, feats[at, :]).astype(BF16)

    step1(1)

    rows_id = lax.broadcasted_iota(jnp.int32, (512, 64), 0)
    owner = (
        ((rows_id // 128) % 2) * 32 + ((rows_id // 64) % 2) * 16 + ((rows_id // 8) % 8) * 2 + rows_id // 256
    )
    repeat = (owner == lax.broadcasted_iota(jnp.int32, (512, 64), 1)).astype(F32).astype(BF16)
    first_bin = nn(repeat, exon[0].astype(F32).astype(BF16))
    end_bin = nn(repeat, exon[1].astype(F32).astype(BF16))
    gene = nn(repeat, exon[2].astype(F32).astype(BF16))
    step1(2)
    for blk in range(8):
        at = slice(blk * 64, blk * 64 + 64)
        bins = lax.broadcasted_iota(jnp.int32, (64, BINS), 1).astype(F32)
        which = (lax.broadcasted_iota(jnp.int32, (64, 1), 0) % 8).astype(F32)
        total = jnp.zeros((64, BINS), F32)
        for j in range(8):
            lo = jnp.where(gene[at, j : j + 1] == which, first_bin[at, j : j + 1], 1024.0)
            inside = jnp.logical_and(bins >= lo, bins < end_bin[at, j : j + 1])
            total = total + jnp.where(inside, 1.0, 0.0)
        gmat[at, :] = total.astype(BF16)
        if blk == 3:
            step1(3)
    step1(4)
    step1(5)
    step2(0)
    keep1.wait()
    rest1()

    @pl.loop(0, P1 // 256)
    def _(n):
        at = pl.ds(pl.multiple_of(n * 256, 256), 256)
        y[:, at] = nn(ft[...], w1[:, at])

    t_row = lax.broadcasted_iota(jnp.int32, (BINS, 128), 0)
    lane = lax.broadcasted_iota(jnp.int32, (1, 128), 1)

    def shifted(x, tap):
        by = (tap - TAPS // 2) * STEP
        if by == 0:
            return x
        moved = pltpu.roll(x, (BINS - by) % BINS, 0)
        ok = jnp.logical_and(t_row + by >= 0, t_row + by < BINS)
        return jnp.where(ok, moved, 0.0)

    wide = shifted(y[:, 0:128], 0)
    for tap in range(1, TAPS):
        wide = wide + shifted(y[:, tap * 128 : tap * 128 + 128], tap)
    pairs = [y[:, 640 + i * 128 : 768 + i * 128] for i in range(3)]
    even = shifted(pairs[0], 0) + shifted(pairs[1], 2) + shifted(pairs[2], 4)
    odd = shifted(pairs[0], 1) + shifted(pairs[1], 3)
    narrow = even + pltpu.roll(odd, 64, 1)
    r0, r1, r2 = cbias[0:1, :], cbias[1:2, :], cbias[2:3, :]
    low = lane < 64
    wide_bias = jnp.where(b == 0, r0, pltpu.roll(jnp.where(low, r2, r1), 64, 1))
    narrow_bias = jnp.where(b == 0, r1, pltpu.roll(r2, 64, 1))
    wide = gelu(wide + wide_bias).T
    narrow = gelu(narrow + narrow_bias).T
    base = pl.multiple_of(q * COLS, COLS)
    gx[pl.ds(base, 128), :] = (feats[pl.ds(base, 128), :].astype(F32) + wide).astype(BF16)
    base2 = pl.multiple_of(q * COLS + 128, 64)
    gx[pl.ds(base2, 64), :] = (feats[pl.ds(base2, 64), :].astype(F32) + narrow[:64]).astype(BF16)

    start_x, first_x, second_x, third_x, flush_x = gather(gx, 0)
    start_a, first_a, second_a, third_a, flush_a = gather(ga, 1)
    start_r, first_r, second_r, third_r, flush_r = gather(gr, 2)

    start_x()
    step2(1)
    wqt[...] = nt(eye[:128, :128], w1[:, 896:1024]).astype(BF16)
    step2(2)
    first_x()
    step2(3)
    second_x()
    step2(4)
    step2(5)
    keep2.wait()
    rest2()
    wo_step(0)

    @pl.loop(0, P2 // 256)
    def _(n):
        at = pl.ds(pl.multiple_of(n * 256, 256), 256)
        w2t[at, :] = nt(eye, w2[:, at]).astype(BF16)

    wo_step(1)
    third_x()

    qq = nn(wqt[...], gx[...])[64:128].astype(BF16)
    kv = nn(w2t[0:256, :], gx[...]).astype(BF16)
    scores = tn(kv[0:64], qq) * (1.0 / math.sqrt(KEY))
    weights = jnp.exp(scores)
    prob = (weights / jnp.sum(weights, axis=0, keepdims=True)).astype(BF16)
    ga[pl.ds(base, COLS), :] = nn(kv[64:256], prob).astype(BF16)

    start_a()
    wo_step(2)
    first_a()
    wo_step(3)
    second_a()
    wo_step(4)
    wo_step(5)
    wo_rest()
    third_a()

    resid = gx[pl.ds(base, COLS), :].astype(F32) + nn(wo[...], ga[...])
    gr[pl.ds(base, COLS), :] = resid.astype(BF16)
    start_r()
    first_r()
    second_r()
    third_r()

    for blk in range(TRK // 256):
        logits = nn(w2t[256 + blk * 256 : 512 + blk * 256, :], gr[...])
        bias = hbias[pl.ds(pl.multiple_of(b * TRK + blk * 256, 256), 256), :]
        logits = logits + bias
        soft = jnp.maximum(logits, 0.0) + jnp.log1p(jnp.exp(-jnp.abs(logits)))
        trk[blk * 256 : blk * 256 + 256, :] = soft.astype(BF16)

    def sums(core):
        rows = gmat[pl.ds(pl.multiple_of(core * 256, 256), 256), :]
        left = nt(rows, trk[0:256, :]).reshape(32, 8, 256)
        right = nt(rows, trk[256:512, :]).reshape(32, 8, 256)
        return jnp.concatenate([left, right], axis=1)

    ex_out[...] = sums(1 - c).astype(BF16)
    swap = remote(ex_out, ex_in, sse.at[0], rse.at[0], to("cp"))
    swap.start()
    own_sums = sums(c)
    swap.wait_recv()
    gs[...] = (own_sums + ex_in[...].astype(F32)).astype(BF16)

    def gene_copy(rel):
        ds, dh, dz = rel // 16, (rel // 8) % 2, rel % 8
        s2, h2, z2 = (s + ds) % 2, (h + dh) % 2, (z + dz) % NZ
        return remote(
            gs.at[s2 * 16 + h2 * 8 + z2],
            gin.at[rel],
            ssg.at[rel],
            rsg.at[rel],
            (s2, win_of(h2, z2, c), m),
        )

    @pl.loop(1, 32)
    def _(rel):
        gene_copy(rel).start()

    gin[0] = gs[s * 16 + h * 8 + z]

    @pl.loop(1, 32)
    def _(rel):
        gene_copy(rel).wait_recv()

    same = gin[0].astype(F32)
    other = gin[8].astype(F32)
    for rel in range(1, 8):
        same = same + gin[rel].astype(F32)
        other = other + gin[8 + rel].astype(F32)
    for rel in range(8):
        other = other + gin[16 + rel].astype(F32)
        same = same + gin[24 + rel].astype(F32)
    for value, at in ((same, b), (other, 1 - b)):
        value = jnp.log1p(value)
        out[:, pl.ds(pl.multiple_of(at * TRK, TRK), 256)] = value[0:8]
        out[:, pl.ds(pl.multiple_of(at * TRK + 256, 256), 256)] = value[8:16]

    flush1()
    flush2()
    wo_flush()
    flush_x()
    flush_a()
    flush_r()
    swap.wait_send()

    @pl.loop(1, 32)
    def _(rel):
        gene_copy(rel).wait_send()


def local(feats, conv_w, conv_bias, qkv_w, out_w, head_w, head_bias, exon_lists):
    s = lax.axis_index("segment")
    w = lax.axis_index("win")
    b = (s + w // (2 * NZ)) % 2
    conv = lax.dynamic_slice(conv_w, (0, 0, b * COLS), (ROWS, TAPS, COLS))
    qkv = lax.dynamic_slice(qkv_w, (0, b * 320), (ROWS, 320))
    head = lax.dynamic_slice(head_w, (0, b * TRK), (ROWS, TRK))
    p1 = jnp.concatenate(
        [conv[:, :, :128].reshape(ROWS, 640), conv[:, :, 128:].reshape(ROWS, 320), qkv[:, :KEY]], axis=1
    )
    p2 = jnp.concatenate([qkv[:, KEY:], head], axis=1)
    vmem = pl.BlockSpec(memory_space=pltpu.VMEM)
    dma = pltpu.SemaphoreType.DMA
    return pl.pallas_call(
        kernel,
        out_shape=jax.ShapeDtypeStruct((8, 1024), F32),
        in_specs=[vmem] * 7,
        out_specs=vmem,
        scratch_shapes=[
            pltpu.VMEM((D, P1), BF16),
            pltpu.VMEM((D, P2), BF16),
            pltpu.VMEM((COLS, D), BF16),
            pltpu.VMEM((D, BINS), BF16),
            pltpu.VMEM((D, BINS), BF16),
            pltpu.VMEM((D, BINS), BF16),
            pltpu.VMEM((BINS, D), BF16),
            pltpu.VMEM((BINS, P1), F32),
            pltpu.VMEM((128, D), BF16),
            pltpu.VMEM((P2, D), BF16),
            pltpu.VMEM((TRK, BINS), BF16),
            pltpu.VMEM((512, BINS), BF16),
            pltpu.VMEM((32, 16, 256), BF16),
            pltpu.VMEM((32, 16, 256), BF16),
            pltpu.VMEM((32, 16, 256), BF16),
            pltpu.VMEM((32, 16, 256), BF16),
            dma((32,)), dma((32,)), dma((32,)), dma((32,)), dma((4,)), dma((32,)), dma((4,)), dma((1,)),
            dma((27,)), dma((27,)), dma((32,)), dma((32,)), dma((1,)), dma((1,)), dma((3,)),
        ],
        compiler_params=pltpu.CompilerParams(collective_id=0, has_side_effects=True, vmem_limit_bytes=48 * 1024 * 1024),
    )(
        feats[0], p1, p2, out_w, conv_bias.reshape(3, 128), head_bias.reshape(1024, 1), exon_lists[:, 0],
    )


def solution(mesh):
    in_specs = (
        P("win", None, None),
        P("win", None, "mp"),
        P("mp"),
        P("win", "mp"),
        P("win", "mp"),
        P("win", "mp"),
        P("mp"),
        P(None, "win", None, None),
    )
    return jax.shard_map(
        local, mesh=mesh, in_specs=in_specs, out_specs=P(("segment", "win"), "mp"), check_vma=False
    )
```

```python
import math

import jax
import jax.numpy as jnp
from jax import lax
from jax.experimental import pallas as pl
from jax.experimental.pallas import tpu as pltpu
from jax.sharding import PartitionSpec as P

MESH = pl.DeviceIdType.MESH
F32 = jnp.float32
BF16 = jnp.bfloat16

KEY = 64
VAL = 192
TAPS = 5
STEP = 4
BINS = 256
D = 1536
ROWS = 48
COLS = 192
WIDE = 640
TAIL = 384
KV = 256
TRK = 512
NZ = 8
NY = 4

QUICK = (
    ((("O", 0), ("zp", "zm", "xp", "zp2", "zm2", "cp")),),
    (
        (("O", -1), ("cp",)),
        (("O", 1), ("cp",)),
        (("X", 0), ("zp", "zm", "cp")),
        (("O", -2), ("zp", "xp", "cp")),
        (("O", 2), ("zm", "cp")),
    ),
    (
        (("O", -3), ("zp", "xp", "cp")),
        (("O", 3), ("xp", "cp")),
        (("X", 1), ("zm", "cp")),
        (("X", -1), ("cp",)),
        (("X", -2), ("cp",)),
    ),
    (
        (("O", -4), ("xp", "cp")),
        (("X", 2), ("cp",)),
        (("X", 3), ("cp",)),
        (("X", -3), ("cp",)),
    ),
    ((("X", -4), ("cp",)),),
)
LEAN = (
    ((("O", 0), ("zp", "zm", "xp", "cp")),),
    ((("O", -1), ("zp", "cp")), (("O", 1), ("zm", "cp")), (("X", 0), ("zp", "zm", "cp"))),
    (
        (("O", -2), ("zp", "xp", "cp")),
        (("O", 2), ("zm", "cp")),
        (("X", 1), ("zm", "cp")),
        (("X", -1), ("cp",)),
    ),
    (
        (("O", -3), ("zp", "xp", "cp")),
        (("O", 3), ("xp", "cp")),
        (("X", 2), ("cp",)),
        (("X", -2), ("cp",)),
    ),
    ((("O", -4), ("xp", "cp")), (("X", 3), ("cp",)), (("X", -3), ("cp",))),
    ((("X", -4), ("cp",)),),
)


def nt(left, right):
    return lax.dot_general(left, right, (((1,), (1,)), ((), ())), preferred_element_type=F32)


def nn(left, right):
    return lax.dot_general(left, right, (((1,), (0,)), ((), ())), preferred_element_type=F32)


def tn(left, right):
    return lax.dot_general(left, right, (((0,), (0,)), ((), ())), preferred_element_type=F32)


def gelu(x):
    return 0.5 * x * (1.0 + jnp.tanh(math.sqrt(2.0 / math.pi) * (x + 0.044715 * (x * x * x))))


def kernel(
    feats_h, conv_h, qkv_h, outw_h, head_h, cbias_h, hbias_h, exon_h,
    out,
    feats, conv, qkv, cbias, hbias, exon, pa, pb, pk, ph, po,
    wa, wb, wk, wh, wo, gx, ga, gr, ft, y, wqt, wkt, wht, hcol, trk, gmat, ex_out, ex_in, gs, gin,
    ring_r, ring_s, rsy, ssy, rsa, ssa, rsg, ssg, rse, sse, lsem,
):
    s = lax.axis_index("segment")
    w = lax.axis_index("win")
    m = lax.axis_index("mp")
    h = w // (2 * NZ)
    z = (w // 2) % NZ
    c = w % 2
    b = (s + h) % 2
    q = 2 * m + b

    def win_of(hh, zz, cc):
        return hh * (2 * NZ) + zz * 2 + cc

    where = {
        "zp": {"win": win_of(h, (z + 1) % NZ, c)},
        "zm": {"win": win_of(h, (z + NZ - 1) % NZ, c)},
        "zp2": {"win": win_of(h, (z + 2) % NZ, c)},
        "zm2": {"win": win_of(h, (z + NZ - 2) % NZ, c)},
        "xp": {"segment": 1 - s, "win": win_of(1 - h, z, c)},
        "cp": {"win": win_of(h, z, 1 - c)},
        "sp": {"segment": 1 - s},
        "yp": {"mp": (m + 1) % NY},
        "ym": {"mp": (m + NY - 1) % NY},
        "y2": {"mp": (m + 2) % NY},
    }

    def to(name):
        d = {"segment": s, "win": w, "mp": m}
        d.update(where[name])
        return (d["segment"], d["win"], d["mp"])

    barrier = pltpu.get_barrier_semaphore()
    for name in where:
        pl.semaphore_signal(barrier, inc=1, device_id=to(name), device_id_type=MESH)

    local_copies = [
        pltpu.make_async_copy(src, dst, lsem.at[i])
        for i, (src, dst) in enumerate(
            (
                (conv_h, conv),
                (qkv_h, qkv),
                (feats_h, feats),
                (head_h.at[:, pl.ds(pl.multiple_of(b * TRK, TRK), TRK)], ph),
                (outw_h, po),
                (exon_h, exon),
                (cbias_h, cbias),
                (hbias_h, hbias),
            )
        )
    ]
    for copy in local_copies:
        copy.start()

    def remote(src, dst, send, recv, device):
        return pltpu.make_async_remote_copy(
            src_ref=src, dst_ref=dst, send_sem=send, recv_sem=recv, device_id=device, device_id_type=MESH
        )

    lane = lax.broadcasted_iota(jnp.int32, (1, 128), 1)
    low = lane < 64
    local_copies[0].wait()
    local_copies[1].wait()
    thin = []
    for tap in range(TAPS):
        part = conv[tap].astype(F32)
        part = jnp.where(b == 0, part, pltpu.roll(part, COLS, 1))
        pa[:, tap * 128 : tap * 128 + 128] = part[:, :128].astype(BF16)
        thin.append(part[:, 128:256])
    head_part = qkv[...].astype(F32)
    head_part = jnp.where(b == 0, head_part, pltpu.roll(head_part, 320, 1))
    thin.append(head_part[:, :128])
    for i in range(3):
        pb[:, i * 128 : i * 128 + 128] = jnp.where(low, thin[2 * i], pltpu.roll(thin[2 * i + 1], 64, 1)).astype(BF16)
    pk[...] = pltpu.roll(head_part, 576, 1)[:, :KV].astype(BF16)

    pl.semaphore_wait(barrier, len(where))

    def ring(index, plan, own, buf):
        count = [0]
        tail = []

        def rows(win):
            return buf.at[pl.ds(pl.multiple_of(win * ROWS, ROWS), ROWS), :]

        def shard_win(code, core):
            kind, d = code
            return win_of(h if kind == "O" else 1 - h, (z + d + NZ) % NZ, core)

        def recv(win):
            return ring_r.at[index, win]

        def wait(win):
            remote(rows(win), rows(win), ring_s.at[index, 0], recv(win), to("cp")).wait_recv()

        def step(r):
            for code, names in plan[r]:
                win = shard_win(code, c)
                src = rows(win)
                if code == ("O", 0):
                    src = rows(win) if own is None else own
                else:
                    wait(win)
                for name in names:
                    copy = remote(src, rows(win), ring_s.at[index, count[0]], recv(win), to(name))
                    count[0] += 1
                    copy.start()
                    tail.append(copy)

        def rest():
            for group in plan:
                for code, names in group:
                    wait(shard_win(code, 1 - c))

        def flush():
            for copy in tail:
                copy.wait_send()

        keep = None
        if own is not None:
            keep = pltpu.make_async_copy(own, rows(w), lsem.at[8 + index])
        return step, rest, flush, keep

    def gather(buf, index, lo, n):
        def rows(dm, other, skip=0, count=n):
            slot = 2 * ((m + dm + NY) % NY) + (1 - b if other else b)
            return buf.at[pl.ds(pl.multiple_of(slot * COLS + lo + skip, 16), count), :]

        half = n // 2
        tail = []

        def push(i, ref, name):
            copy = remote(ref, ref, ssa.at[index, i], rsa.at[index, i], to(name))
            copy.start()
            tail.append(copy)

        def got(i, ref):
            remote(ref, ref, ssa.at[index, i], rsa.at[index, i], to("sp")).wait_recv()

        def start():
            own = rows(0, False)
            push(0, own, "yp")
            push(1, own, "ym")
            push(2, own, "sp")

        def first():
            got(0, rows(-1, False))
            push(3, rows(-1, False, 0, half), "yp")
            got(1, rows(1, False))
            push(4, rows(1, False, half, half), "ym")
            got(2, rows(0, True))
            push(5, rows(0, True), "yp")
            push(6, rows(0, True), "ym")

        def second():
            got(3, rows(2, False, 0, half))
            got(4, rows(2, False, half, half))
            push(7, rows(2, False), "sp")

        def third():
            got(5, rows(-1, True))
            got(6, rows(1, True))
            got(7, rows(2, True))

        def flush():
            for copy in tail:
                copy.wait_send()

        return start, first, second, third, flush

    step_a, rest_a, flush_a, keep_a = ring(0, QUICK, pa, wa)
    step_b, rest_b, flush_b, keep_b = ring(1, QUICK, pb, wb)
    step_k, rest_k, flush_k, keep_k = ring(2, QUICK, pk, wk)
    step_h, rest_h, flush_h, keep_h = ring(3, LEAN, ph, wh)
    step_o, rest_o, flush_o, _ = ring(4, LEAN, None, wo)

    step_a(0)
    step_b(0)
    step_k(0)
    keep_a.start()
    keep_b.start()
    keep_k.start()

    def wo_part(model):
        return wo.at[
            pl.ds(pl.multiple_of(w * ROWS, ROWS), ROWS),
            pl.ds(pl.multiple_of(model * 2 * COLS, 2 * COLS), 2 * COLS),
        ]

    for i in range(2, len(local_copies)):
        local_copies[i].wait()
    keep_h.start()
    keep_o = pltpu.make_async_copy(po, wo_part(m), lsem.at[12])
    keep_o.start()
    hops = (("yp", 1), ("ym", 3), ("y2", 2))
    wo_sends = [remote(po, wo_part(m), ssy.at[j], rsy.at[j], to(name)) for name, j in hops]
    for copy in wo_sends:
        copy.start()

    eye = (
        lax.broadcasted_iota(jnp.int32, (BINS, BINS), 0) == lax.broadcasted_iota(jnp.int32, (BINS, BINS), 1)
    ).astype(F32).astype(BF16)

    @pl.loop(0, D // BINS)
    def _(n):
        at = pl.ds(pl.multiple_of(n * BINS, BINS), BINS)
        ft[:, at] = nt(eye, feats[at, :]).astype(BF16)

    step_a(1)
    step_b(1)
    step_k(1)

    rows_id = lax.broadcasted_iota(jnp.int32, (512, 64), 0)
    owner = (
        ((rows_id // 128) % 2) * 32 + ((rows_id // 64) % 2) * 16 + ((rows_id // 8) % 8) * 2 + rows_id // 256
    )
    repeat = (owner == lax.broadcasted_iota(jnp.int32, (512, 64), 1)).astype(F32).astype(BF16)
    first_bin = nt(repeat, exon[0].astype(F32).astype(BF16))
    end_bin = nt(repeat, exon[1].astype(F32).astype(BF16))
    gene = nt(repeat, exon[2].astype(F32).astype(BF16))

    def gene_bins(blk):
        at = slice(blk * 64, blk * 64 + 64)
        bins = lax.broadcasted_iota(jnp.int32, (64, BINS), 1).astype(F32)
        which = (lax.broadcasted_iota(jnp.int32, (64, 1), 0) % 8).astype(F32)
        total = jnp.zeros((64, BINS), F32)
        for j in range(8):
            lo = jnp.where(gene[at, j : j + 1] == which, first_bin[at, j : j + 1], 1024.0)
            inside = jnp.logical_and(bins >= lo, bins < end_bin[at, j : j + 1])
            total = total + jnp.where(inside, 1.0, 0.0)
        gmat[at, :] = total.astype(BF16)

    for blk in range(2):
        gene_bins(blk)
    step_a(2)
    step_b(2)
    step_k(2)
    for blk in range(2, 4):
        gene_bins(blk)
    step_a(3)
    step_b(3)
    step_k(3)
    keep_o.wait()
    for name, j in hops:
        remote(po, wo_part((m - j + NY) % NY), ssy.at[j], rsy.at[j], to("cp")).wait_recv()
    step_h(0)
    step_o(0)
    step_a(4)
    step_b(4)
    keep_a.wait()
    rest_a()

    t_row = lax.broadcasted_iota(jnp.int32, (BINS, 128), 0)

    def shifted(x, tap):
        by = (tap - TAPS // 2) * STEP
        if by == 0:
            return x
        moved = pltpu.roll(x, (BINS - by) % BINS, 0)
        ok = jnp.logical_and(t_row + by >= 0, t_row + by < BINS)
        return jnp.where(ok, moved, 0.0)

    start_x, first_x, second_x, third_x, flush_x = gather(gx, 0, 0, 128)
    start_u, first_u, second_u, third_u, flush_u = gather(gx, 1, 128, 64)
    start_v, first_v, second_v, third_v, flush_v = gather(ga, 2, 0, 96)
    start_w, first_w, second_w, third_w, flush_w = gather(ga, 3, 96, 96)

    c0, c1, c2 = (cbias[i * 128 : i * 128 + 128].reshape(1, 128) for i in range(3))
    wide_bias = jnp.where(b == 0, c0, pltpu.roll(jnp.where(low, c2, c1), 64, 1))
    narrow_bias = jnp.where(b == 0, c1, pltpu.roll(c2, 64, 1))
    base = pl.multiple_of(q * COLS, COLS)
    base2 = pl.multiple_of(q * COLS + 128, 64)

    for i in range(TAPS):
        y[:, i * 128 : i * 128 + 128] = nn(ft[...], wa[:, i * 128 : i * 128 + 128])
    wide = shifted(y[:, 0:128], 0)
    for tap in range(1, TAPS):
        wide = wide + shifted(y[:, tap * 128 : tap * 128 + 128], tap)
    wide = gelu(wide + wide_bias).T
    gx[pl.ds(base, 128), :] = (feats[pl.ds(base, 128), :].astype(F32) + wide).astype(BF16)
    start_x()

    keep_b.wait()
    rest_b()
    pairs = [nn(ft[...], wb[:, i * 128 : i * 128 + 128]) for i in range(3)]
    even = shifted(pairs[0], 0) + shifted(pairs[1], 2) + shifted(pairs[2], 4)
    odd = shifted(pairs[0], 1) + shifted(pairs[1], 3)
    narrow = even + pltpu.roll(odd, 64, 1)
    narrow = gelu(narrow + narrow_bias).T
    gx[pl.ds(base2, 64), :] = (feats[pl.ds(base2, 64), :].astype(F32) + narrow[:64]).astype(BF16)
    start_u()

    step_k(4)
    keep_k.wait()
    step_h(1)
    step_o(1)
    first_x()
    first_u()
    step_h(2)
    step_o(2)
    rest_k()
    wqt[...] = nt(eye[:128, :128], wb[:, 256:384]).astype(BF16)
    wkt[...] = nt(eye, wk[...]).astype(BF16)
    second_x()
    second_u()
    step_h(3)
    third_x()
    third_u()

    qq = nn(wqt[...], gx[...])[64:128].astype(BF16)
    kv = nn(wkt[...], gx[...]).astype(BF16)
    scores = tn(kv[0:64], qq) * (1.0 / math.sqrt(KEY))
    weights = jnp.exp(scores)
    prob = (weights / jnp.sum(weights, axis=0, keepdims=True)).astype(BF16)
    ga[pl.ds(base, COLS), :] = nn(kv[64:256], prob).astype(BF16)

    start_v()
    start_w()
    step_o(3)
    step_h(4)
    for blk in range(4, 8):
        gene_bins(blk)
    first_v()
    first_w()
    step_o(4)
    step_h(5)
    keep_h.wait()
    rest_h()
    flush_a()
    flush_b()
    second_v()
    second_w()
    for i in range(TRK // 256):
        wht[i * 256 : i * 256 + 256, :] = nt(eye, wh[:, i * 256 : i * 256 + 256]).astype(BF16)
    eye_f = (
        lax.broadcasted_iota(jnp.int32, (128, 128), 0) == lax.broadcasted_iota(jnp.int32, (128, 128), 1)
    )
    for i in range(TRK // 128):
        row = jnp.where(b == 0, hbias[i : i + 1, :], hbias[4 + i : 5 + i, :])
        hcol[i * 128 : i * 128 + 128, :] = jnp.sum(jnp.where(eye_f, row, 0.0), axis=1, keepdims=True)
    step_o(5)
    third_v()
    third_w()
    rest_o()

    for i in range(D // 256):
        at = slice(i * 256, i * 256 + 256)
        gr[at, :] = (gx[at, :].astype(F32) + nn(wo[at, :], ga[...])).astype(BF16)

    for blk in range(TRK // 256):
        at = slice(blk * 256, blk * 256 + 256)
        logits = nn(wht[at, :], gr[...]) + hcol[at, :]
        soft = jnp.maximum(logits, 0.0) + jnp.log1p(jnp.exp(-jnp.abs(logits)))
        trk[at, :] = soft.astype(BF16)

    def sums(core):
        rows = gmat[pl.ds(pl.multiple_of(core * 256, 256), 256), :]
        left = nt(rows, trk[0:256, :]).reshape(32, 8, 256)
        right = nt(rows, trk[256:512, :]).reshape(32, 8, 256)
        return jnp.concatenate([left, right], axis=1)

    ex_out[...] = sums(1 - c).astype(BF16)
    swap = remote(ex_out, ex_in, sse.at[0], rse.at[0], to("cp"))
    swap.start()
    own_sums = sums(c)
    swap.wait_recv()
    gs[...] = (own_sums + ex_in[...].astype(F32)).astype(BF16)

    def gene_copy(rel):
        ds, dh, dz = rel // 16, (rel // 8) % 2, rel % 8
        s2, h2, z2 = (s + ds) % 2, (h + dh) % 2, (z + dz) % NZ
        return remote(
            gs.at[s2 * 16 + h2 * 8 + z2],
            gin.at[rel],
            ssg.at[rel],
            rsg.at[rel],
            (s2, win_of(h2, z2, c), m),
        )

    @pl.loop(1, 32)
    def _(rel):
        gene_copy(rel).start()

    gin[0] = gs[s * 16 + h * 8 + z]
    flush_k()
    flush_h()
    flush_o()
    flush_x()
    flush_u()
    flush_v()
    flush_w()
    for copy in wo_sends:
        copy.wait_send()
    swap.wait_send()

    @pl.loop(1, 32)
    def _(rel):
        gene_copy(rel).wait()

    same = gin[0].astype(F32)
    other = gin[8].astype(F32)
    for rel in range(1, 8):
        same = same + gin[rel].astype(F32)
        other = other + gin[8 + rel].astype(F32)
    for rel in range(8):
        other = other + gin[16 + rel].astype(F32)
        same = same + gin[24 + rel].astype(F32)
    for value, at in ((same, b), (other, 1 - b)):
        value = jnp.log1p(value)
        out[:, pl.ds(pl.multiple_of(at * TRK, TRK), 256)] = value[0:8]
        out[:, pl.ds(pl.multiple_of(at * TRK + 256, 256), 256)] = value[8:16]


def local(feats, conv_w, conv_bias, qkv_w, out_w, head_w, head_bias, exon_lists):
    vmem = pltpu.VMEM
    dma = pltpu.SemaphoreType.DMA
    anywhere = pl.BlockSpec(memory_space=pltpu.HBM)
    return pl.pallas_call(
        kernel,
        out_shape=jax.ShapeDtypeStruct((8, 1024), F32),
        in_specs=[anywhere] * 8,
        out_specs=pl.BlockSpec(memory_space=pltpu.VMEM),
        scratch_shapes=[
            vmem((D, BINS), BF16),
            vmem((TAPS, ROWS, 2 * COLS), BF16),
            vmem((ROWS, 640), BF16),
            vmem((384,), F32),
            vmem((8, 128), F32),
            vmem((3, 8, 64), jnp.int32),
            vmem((ROWS, WIDE), BF16),
            vmem((ROWS, TAIL), BF16),
            vmem((ROWS, KV), BF16),
            vmem((ROWS, TRK), BF16),
            vmem((ROWS, 2 * COLS), BF16),
            vmem((D, WIDE), BF16),
            vmem((D, TAIL), BF16),
            vmem((D, KV), BF16),
            vmem((D, TRK), BF16),
            vmem((D, D), BF16),
            vmem((D, BINS), BF16),
            vmem((D, BINS), BF16),
            vmem((D, BINS), BF16),
            vmem((BINS, D), BF16),
            vmem((BINS, WIDE), F32),
            vmem((128, D), BF16),
            vmem((KV, D), BF16),
            vmem((TRK, D), BF16),
            vmem((TRK, 1), F32),
            vmem((TRK, BINS), BF16),
            vmem((512, BINS), BF16),
            vmem((32, 16, 256), BF16),
            vmem((32, 16, 256), BF16),
            vmem((32, 16, 256), BF16),
            vmem((32, 16, 256), BF16),
            dma((5, 32)), dma((5, 34)), dma((4,)), dma((4,)),
            dma((4, 8)), dma((4, 8)), dma((32,)), dma((32,)), dma((1,)), dma((1,)), dma((13,)),
        ],
        compiler_params=pltpu.CompilerParams(
            collective_id=0, has_side_effects=True, vmem_limit_bytes=60 * 1024 * 1024
        ),
    )(
        feats[0],
        conv_w.transpose(1, 0, 2),
        qkv_w,
        out_w,
        head_w,
        conv_bias,
        head_bias.reshape(8, 128),
        exon_lists[:, 0].transpose(0, 2, 1),
    )


def solution(mesh):
    in_specs = (
        P("win", None, None),
        P("win", None, "mp"),
        P("mp"),
        P("win", "mp"),
        P("win", "mp"),
        P("win", "mp"),
        P("mp"),
        P(None, "win", None, None),
    )
    return jax.shard_map(
        local, mesh=mesh, in_specs=in_specs, out_specs=P(("segment", "win"), "mp"), check_vma=False
    )
```

```python
import math

import jax
import jax.numpy as jnp
from jax import lax
from jax.experimental import pallas as pl
from jax.experimental.pallas import tpu as pltpu
from jax.sharding import PartitionSpec as P

MESH = pl.DeviceIdType.MESH
F32 = jnp.float32
BF16 = jnp.bfloat16

KEY = 64
VAL = 192
TAPS = 5
STEP = 4
BINS = 256
D = 1536
ROWS = 48
COLS = 192
WIDE = 640
TAIL = 384
KV = 256
TRK = 512
NZ = 8
NY = 4

QUICK = (
    ((("O", 0), ("zp", "zm", "xp", "zp2", "zm2", "cp")),),
    (
        (("O", -1), ("cp",)),
        (("O", 1), ("cp",)),
        (("X", 0), ("zp", "zm", "cp")),
        (("O", -2), ("zp", "xp", "cp")),
        (("O", 2), ("zm", "cp")),
    ),
    (
        (("O", -3), ("zp", "xp", "cp")),
        (("O", 3), ("xp", "cp")),
        (("X", 1), ("zm", "cp")),
        (("X", -1), ("cp",)),
        (("X", -2), ("cp",)),
    ),
    (
        (("O", -4), ("xp", "cp")),
        (("X", 2), ("cp",)),
        (("X", 3), ("cp",)),
        (("X", -3), ("cp",)),
    ),
    ((("X", -4), ("cp",)),),
)
LEAN = (
    ((("O", 0), ("zp", "zm", "xp", "cp")),),
    ((("O", -1), ("zp", "cp")), (("O", 1), ("zm", "cp")), (("X", 0), ("zp", "zm", "cp"))),
    (
        (("O", -2), ("zp", "xp", "cp")),
        (("O", 2), ("zm", "cp")),
        (("X", 1), ("zm", "cp")),
        (("X", -1), ("cp",)),
    ),
    (
        (("O", -3), ("zp", "xp", "cp")),
        (("O", 3), ("xp", "cp")),
        (("X", 2), ("cp",)),
        (("X", -2), ("cp",)),
    ),
    ((("O", -4), ("xp", "cp")), (("X", 3), ("cp",)), (("X", -3), ("cp",))),
    ((("X", -4), ("cp",)),),
)


def nt(left, right):
    return lax.dot_general(left, right, (((1,), (1,)), ((), ())), preferred_element_type=F32)


def nn(left, right):
    return lax.dot_general(left, right, (((1,), (0,)), ((), ())), preferred_element_type=F32)


def tn(left, right):
    return lax.dot_general(left, right, (((0,), (0,)), ((), ())), preferred_element_type=F32)


def gelu(x):
    return 0.5 * x * (1.0 + jnp.tanh(math.sqrt(2.0 / math.pi) * (x + 0.044715 * (x * x * x))))


def kernel(
    feats_h, conv_h, qkv_h, outw_h, head_h, cbias_h, hbias_h, exon_h,
    out,
    feats, conv, qkv, cbias, hbias, exon, pa, pb, pk, ph, po,
    wa, wb, wk, wh, wo, wo2, gx, ga, gr, ft, y, wqt, wkt, wht, hcol, trk, gmat, ex_out, ex_in, gs, gin,
    ring_r, ring_s, rsy, ssy, rsa, ssa, rsg, ssg, rse, sse, lsem,
):
    s = lax.axis_index("segment")
    w = lax.axis_index("win")
    m = lax.axis_index("mp")
    h = w // (2 * NZ)
    z = (w // 2) % NZ
    c = w % 2
    b = (s + h) % 2
    q = 2 * m + b

    def win_of(hh, zz, cc):
        return hh * (2 * NZ) + zz * 2 + cc

    where = {
        "zp": {"win": win_of(h, (z + 1) % NZ, c)},
        "zm": {"win": win_of(h, (z + NZ - 1) % NZ, c)},
        "zp2": {"win": win_of(h, (z + 2) % NZ, c)},
        "zm2": {"win": win_of(h, (z + NZ - 2) % NZ, c)},
        "xp": {"segment": 1 - s, "win": win_of(1 - h, z, c)},
        "cp": {"win": win_of(h, z, 1 - c)},
        "sp": {"segment": 1 - s},
        "yp": {"mp": (m + 1) % NY},
        "ym": {"mp": (m + NY - 1) % NY},
        "y2": {"mp": (m + 2) % NY},
    }

    def to(name):
        d = {"segment": s, "win": w, "mp": m}
        d.update(where[name])
        return (d["segment"], d["win"], d["mp"])

    barrier = pltpu.get_barrier_semaphore()
    for name in where:
        pl.semaphore_signal(barrier, inc=1, device_id=to(name), device_id_type=MESH)

    local_copies = [
        pltpu.make_async_copy(src, dst, lsem.at[i])
        for i, (src, dst) in enumerate(
            (
                (conv_h, conv),
                (qkv_h, qkv),
                (feats_h, feats),
                (head_h.at[:, pl.ds(pl.multiple_of(b * TRK, TRK), TRK)], ph),
                (outw_h, po),
                (exon_h, exon),
                (cbias_h, cbias),
                (hbias_h, hbias),
            )
        )
    ]
    for copy in local_copies:
        copy.start()

    def remote(src, dst, send, recv, device):
        return pltpu.make_async_remote_copy(
            src_ref=src, dst_ref=dst, send_sem=send, recv_sem=recv, device_id=device, device_id_type=MESH
        )

    lane = lax.broadcasted_iota(jnp.int32, (1, 128), 1)
    low = lane < 64
    local_copies[0].wait()
    local_copies[1].wait()
    thin = []
    for tap in range(TAPS):
        part = conv[tap].astype(F32)
        part = jnp.where(b == 0, part, pltpu.roll(part, COLS, 1))
        pa[:, tap * 128 : tap * 128 + 128] = part[:, :128].astype(BF16)
        thin.append(part[:, 128:256])
    head_part = qkv[...].astype(F32)
    head_part = jnp.where(b == 0, head_part, pltpu.roll(head_part, 320, 1))
    thin.append(head_part[:, :128])
    for i in range(3):
        pb[:, i * 128 : i * 128 + 128] = jnp.where(low, thin[2 * i], pltpu.roll(thin[2 * i + 1], 64, 1)).astype(BF16)
    pk[...] = pltpu.roll(head_part, 576, 1)[:, :KV].astype(BF16)

    pl.semaphore_wait(barrier, len(where))

    def ring(index, plan, own, buf):
        count = [0]
        tail = []

        def rows(win):
            return buf.at[pl.ds(pl.multiple_of(win * ROWS, ROWS), ROWS), :]

        def shard_win(code, core):
            kind, d = code
            return win_of(h if kind == "O" else 1 - h, (z + d + NZ) % NZ, core)

        def recv(win):
            return ring_r.at[index, win]

        def wait(win):
            remote(rows(win), rows(win), ring_s.at[index, 0], recv(win), to("cp")).wait_recv()

        def step(r):
            for code, names in plan[r]:
                win = shard_win(code, c)
                src = rows(win)
                if code == ("O", 0):
                    src = rows(win) if own is None else own
                else:
                    wait(win)
                for name in names:
                    copy = remote(src, rows(win), ring_s.at[index, count[0]], recv(win), to(name))
                    count[0] += 1
                    copy.start()
                    tail.append(copy)

        def rest():
            for group in plan:
                for code, names in group:
                    wait(shard_win(code, 1 - c))

        def flush():
            for copy in tail:
                copy.wait_send()

        keep = None
        if own is not None:
            keep = pltpu.make_async_copy(own, rows(w), lsem.at[8 + index])
        return step, rest, flush, keep

    def gather(buf, index, lo, n):
        def rows(dm, other, skip=0, count=n):
            slot = 2 * ((m + dm + NY) % NY) + (1 - b if other else b)
            return buf.at[pl.ds(pl.multiple_of(slot * COLS + lo + skip, 16), count), :]

        half = n // 2
        tail = []

        def push(i, ref, name):
            copy = remote(ref, ref, ssa.at[index, i], rsa.at[index, i], to(name))
            copy.start()
            tail.append(copy)

        def got(i, ref):
            remote(ref, ref, ssa.at[index, i], rsa.at[index, i], to("sp")).wait_recv()

        def start():
            own = rows(0, False)
            push(0, own, "yp")
            push(1, own, "ym")
            push(2, own, "sp")

        def first():
            got(0, rows(-1, False))
            push(3, rows(-1, False, 0, half), "yp")
            got(1, rows(1, False))
            push(4, rows(1, False, half, half), "ym")
            got(2, rows(0, True))
            push(5, rows(0, True), "yp")
            push(6, rows(0, True), "ym")

        def second():
            got(3, rows(2, False, 0, half))
            got(4, rows(2, False, half, half))
            push(7, rows(2, False), "sp")

        def third():
            got(5, rows(-1, True))
            got(6, rows(1, True))
            got(7, rows(2, True))

        def flush():
            for copy in tail:
                copy.wait_send()

        return start, first, second, third, flush

    step_a, rest_a, flush_a, keep_a = ring(0, QUICK, pa, wa)
    step_b, rest_b, flush_b, keep_b = ring(1, QUICK, pb, wb)
    step_k, rest_k, flush_k, keep_k = ring(2, QUICK, pk, wk)
    step_h, rest_h, flush_h, keep_h = ring(3, LEAN, ph, wh)
    step_o, rest_o, flush_o, _ = ring(4, LEAN, None, wo)
    step_p, rest_p, flush_p, _ = ring(5, LEAN, None, wo2)

    step_a(0)
    step_b(0)
    keep_a.start()
    keep_b.start()
    keep_k.start()

    def wo_part(buf, model):
        return buf.at[
            pl.ds(pl.multiple_of(w * ROWS, ROWS), ROWS),
            pl.ds(pl.multiple_of((model % 2) * 2 * COLS, 2 * COLS), 2 * COLS),
        ]

    for i in range(2, len(local_copies)):
        local_copies[i].wait()
    keep_h.start()

    def each_part(model, act):
        @pl.when(model < 2)
        def _():
            act(wo_part(wo, model))

        @pl.when(model >= 2)
        def _():
            act(wo_part(wo2, model))

    hops = (("yp", 1), ("ym", 3), ("y2", 2))
    each_part(m, lambda ref: pltpu.make_async_copy(po, ref, lsem.at[12]).start())
    for name, j in hops:
        each_part(m, lambda ref, name=name, j=j: remote(po, ref, ssy.at[j], rsy.at[j], to(name)).start())

    def wo_ready():
        each_part(m, lambda ref: pltpu.make_async_copy(po, ref, lsem.at[12]).wait())
        for name, j in hops:
            each_part(
                (m - j + NY) % NY, lambda ref, j=j: remote(po, ref, ssy.at[j], rsy.at[j], to("cp")).wait_recv()
            )

    eye = (
        lax.broadcasted_iota(jnp.int32, (BINS, BINS), 0) == lax.broadcasted_iota(jnp.int32, (BINS, BINS), 1)
    ).astype(F32).astype(BF16)

    @pl.loop(0, D // BINS)
    def _(n):
        at = pl.ds(pl.multiple_of(n * BINS, BINS), BINS)
        ft[:, at] = nt(eye, feats[at, :]).astype(BF16)

    step_a(1)
    step_b(1)
    step_k(0)

    rows_id = lax.broadcasted_iota(jnp.int32, (512, 64), 0)
    owner = (
        ((rows_id // 128) % 2) * 32 + ((rows_id // 64) % 2) * 16 + ((rows_id // 8) % 8) * 2 + rows_id // 256
    )
    repeat = (owner == lax.broadcasted_iota(jnp.int32, (512, 64), 1)).astype(F32).astype(BF16)
    first_bin = nt(repeat, exon[0].astype(F32).astype(BF16))
    end_bin = nt(repeat, exon[1].astype(F32).astype(BF16))
    gene = nt(repeat, exon[2].astype(F32).astype(BF16))

    def gene_bins(blk):
        at = slice(blk * 64, blk * 64 + 64)
        bins = lax.broadcasted_iota(jnp.int32, (64, BINS), 1).astype(F32)
        which = (lax.broadcasted_iota(jnp.int32, (64, 1), 0) % 8).astype(F32)
        total = jnp.zeros((64, BINS), F32)
        for j in range(8):
            lo = jnp.where(gene[at, j : j + 1] == which, first_bin[at, j : j + 1], 1024.0)
            inside = jnp.logical_and(bins >= lo, bins < end_bin[at, j : j + 1])
            total = total + jnp.where(inside, 1.0, 0.0)
        gmat[at, :] = total.astype(BF16)

    for blk in range(2):
        gene_bins(blk)
    step_a(2)
    step_b(2)
    step_k(1)
    for blk in range(2, 4):
        gene_bins(blk)
    step_a(3)
    step_b(3)
    step_k(2)
    step_h(0)
    step_a(4)
    step_b(4)
    wo_ready()
    step_o(0)
    step_p(0)
    keep_a.wait()
    rest_a()

    t_row = lax.broadcasted_iota(jnp.int32, (BINS, 128), 0)

    def shifted(x, tap):
        by = (tap - TAPS // 2) * STEP
        if by == 0:
            return x
        moved = pltpu.roll(x, (BINS - by) % BINS, 0)
        ok = jnp.logical_and(t_row + by >= 0, t_row + by < BINS)
        return jnp.where(ok, moved, 0.0)

    start_x, first_x, second_x, third_x, flush_x = gather(gx, 0, 0, 128)
    start_u, first_u, second_u, third_u, flush_u = gather(gx, 1, 128, 64)
    start_v, first_v, second_v, third_v, flush_v = gather(ga, 2, 0, 96)
    start_w, first_w, second_w, third_w, flush_w = gather(ga, 3, 96, 96)

    c0, c1, c2 = (cbias[i * 128 : i * 128 + 128].reshape(1, 128) for i in range(3))
    wide_bias = jnp.where(b == 0, c0, pltpu.roll(jnp.where(low, c2, c1), 64, 1))
    narrow_bias = jnp.where(b == 0, c1, pltpu.roll(c2, 64, 1))
    base = pl.multiple_of(q * COLS, COLS)
    base2 = pl.multiple_of(q * COLS + 128, 64)

    for i in range(TAPS):
        y[:, i * 128 : i * 128 + 128] = nn(ft[...], wa[:, i * 128 : i * 128 + 128])
    wide = shifted(y[:, 0:128], 0)
    for tap in range(1, TAPS):
        wide = wide + shifted(y[:, tap * 128 : tap * 128 + 128], tap)
    wide = gelu(wide + wide_bias).T
    gx[pl.ds(base, 128), :] = (feats[pl.ds(base, 128), :].astype(F32) + wide).astype(BF16)
    start_x()

    keep_b.wait()
    rest_b()
    pairs = [nn(ft[...], wb[:, i * 128 : i * 128 + 128]) for i in range(3)]
    even = shifted(pairs[0], 0) + shifted(pairs[1], 2) + shifted(pairs[2], 4)
    odd = shifted(pairs[0], 1) + shifted(pairs[1], 3)
    narrow = even + pltpu.roll(odd, 64, 1)
    narrow = gelu(narrow + narrow_bias).T
    gx[pl.ds(base2, 64), :] = (feats[pl.ds(base2, 64), :].astype(F32) + narrow[:64]).astype(BF16)
    start_u()

    step_k(3)
    step_h(1)
    step_o(1)
    step_p(1)
    first_x()
    first_u()
    step_k(4)
    step_h(2)
    step_o(2)
    keep_k.wait()
    wqt[...] = nt(eye[:128, :128], wb[:, 256:384]).astype(BF16)
    second_x()
    second_u()
    step_p(2)
    rest_k()
    wkt[...] = nt(eye, wk[...]).astype(BF16)
    third_x()
    third_u()

    qq = nn(wqt[...], gx[...])[64:128].astype(BF16)
    kv = nn(wkt[...], gx[...]).astype(BF16)
    scores = tn(kv[0:64], qq) * (1.0 / math.sqrt(KEY))
    weights = jnp.exp(scores)
    prob = (weights / jnp.sum(weights, axis=0, keepdims=True)).astype(BF16)
    ga[pl.ds(base, COLS), :] = nn(kv[64:256], prob).astype(BF16)

    start_v()
    start_w()
    step_h(3)
    step_o(3)
    step_p(3)
    for blk in range(4, 8):
        gene_bins(blk)
    first_v()
    first_w()
    step_h(4)
    step_o(4)
    step_p(4)
    flush_a()
    flush_b()
    second_v()
    second_w()
    step_h(5)
    step_o(5)
    step_p(5)
    keep_h.wait()
    rest_h()
    for i in range(TRK // 256):
        wht[i * 256 : i * 256 + 256, :] = nt(eye, wh[:, i * 256 : i * 256 + 256]).astype(BF16)
    eye_f = (
        lax.broadcasted_iota(jnp.int32, (128, 128), 0) == lax.broadcasted_iota(jnp.int32, (128, 128), 1)
    )
    for i in range(TRK // 128):
        row = jnp.where(b == 0, hbias[i : i + 1, :], hbias[4 + i : 5 + i, :])
        hcol[i * 128 : i * 128 + 128, :] = jnp.sum(jnp.where(eye_f, row, 0.0), axis=1, keepdims=True)
    third_v()
    third_w()
    rest_o()
    rest_p()

    for i in range(D // 256):
        at = slice(i * 256, i * 256 + 256)
        gr[at, :] = (gx[at, :].astype(F32) + (nn(wo[at, :], ga[0 : D // 2, :]) + nn(wo2[at, :], ga[D // 2 :, :]))).astype(BF16)

    def sums(core, blk):
        rows = gmat[pl.ds(pl.multiple_of(core * 256, 256), 256), :]
        return nt(rows, trk[blk * 256 : blk * 256 + 256, :]).reshape(32, 8, 256)

    swaps = []
    for blk in range(TRK // 256):
        at = slice(blk * 256, blk * 256 + 256)
        logits = nn(wht[at, :], gr[...]) + hcol[at, :]
        soft = jnp.maximum(logits, 0.0) + jnp.log1p(jnp.exp(-jnp.abs(logits)))
        trk[at, :] = soft.astype(BF16)
        give = sums(1 - c, blk)
        ex_out[blk] = jnp.concatenate([give[:, :, :128], give[:, :, 128:]], axis=1).astype(BF16)
        swaps.append(remote(ex_out.at[blk], ex_in.at[blk], sse.at[blk], rse.at[blk], to("cp")))
        swaps[blk].start()
    keep_sums = [sums(c, blk) for blk in range(TRK // 256)]
    for blk in range(TRK // 256):
        swaps[blk].wait_recv()
        took = ex_in[blk].astype(F32)
        keep_sums[blk] = keep_sums[blk] + jnp.concatenate([took[:, :8], took[:, 8:]], axis=2)
    gs[...] = jnp.concatenate(keep_sums, axis=1).astype(BF16)

    def gene_copy(rel):
        ds, dh, dz = rel // 16, (rel // 8) % 2, rel % 8
        s2, h2, z2 = (s + ds) % 2, (h + dh) % 2, (z + dz) % NZ
        return remote(
            gs.at[s2 * 16 + h2 * 8 + z2],
            gin.at[rel],
            ssg.at[rel],
            rsg.at[rel],
            (s2, win_of(h2, z2, c), m),
        )

    gene_copies = [gene_copy(part * 8 + dz) for dz in (4, 3, 5, 2, 6, 1, 7, 0) for part in (3, 2, 1, 0) if part + dz]
    for copy in gene_copies:
        copy.start()

    gin[0] = gs[s * 16 + h * 8 + z]
    flush_k()
    flush_h()
    flush_o()
    flush_p()
    flush_x()
    flush_u()
    flush_v()
    flush_w()
    for name, j in hops:
        each_part(m, lambda ref, name=name, j=j: remote(po, ref, ssy.at[j], rsy.at[j], to(name)).wait_send())
    for swap in swaps:
        swap.wait_send()
    for copy in gene_copies:
        copy.wait()

    same = gin[0].astype(F32)
    other = gin[8].astype(F32)
    for rel in range(1, 8):
        same = same + gin[rel].astype(F32)
        other = other + gin[8 + rel].astype(F32)
    for rel in range(8):
        other = other + gin[16 + rel].astype(F32)
        same = same + gin[24 + rel].astype(F32)
    for value, at in ((same, b), (other, 1 - b)):
        value = jnp.log1p(value)
        out[:, pl.ds(pl.multiple_of(at * TRK, TRK), 256)] = value[0:8]
        out[:, pl.ds(pl.multiple_of(at * TRK + 256, 256), 256)] = value[8:16]


def local(feats, conv_w, conv_bias, qkv_w, out_w, head_w, head_bias, exon_lists):
    vmem = pltpu.VMEM
    dma = pltpu.SemaphoreType.DMA
    anywhere = pl.BlockSpec(memory_space=pltpu.HBM)
    return pl.pallas_call(
        kernel,
        out_shape=jax.ShapeDtypeStruct((8, 1024), F32),
        in_specs=[anywhere] * 8,
        out_specs=pl.BlockSpec(memory_space=pltpu.VMEM),
        scratch_shapes=[
            vmem((D, BINS), BF16),
            vmem((TAPS, ROWS, 2 * COLS), BF16),
            vmem((ROWS, 640), BF16),
            vmem((384,), F32),
            vmem((8, 128), F32),
            vmem((3, 8, 64), jnp.int32),
            vmem((ROWS, WIDE), BF16),
            vmem((ROWS, TAIL), BF16),
            vmem((ROWS, KV), BF16),
            vmem((ROWS, TRK), BF16),
            vmem((ROWS, 2 * COLS), BF16),
            vmem((D, WIDE), BF16),
            vmem((D, TAIL), BF16),
            vmem((D, KV), BF16),
            vmem((D, TRK), BF16),
            vmem((D, D // 2), BF16),
            vmem((D, D // 2), BF16),
            vmem((D, BINS), BF16),
            vmem((D, BINS), BF16),
            vmem((D, BINS), BF16),
            vmem((BINS, D), BF16),
            vmem((BINS, WIDE), F32),
            vmem((128, D), BF16),
            vmem((KV, D), BF16),
            vmem((TRK, D), BF16),
            vmem((TRK, 1), F32),
            vmem((TRK, BINS), BF16),
            vmem((512, BINS), BF16),
            vmem((2, 32, 16, 128), BF16),
            vmem((2, 32, 16, 128), BF16),
            vmem((32, 16, 256), BF16),
            vmem((32, 16, 256), BF16),
            dma((6, 32)), dma((6, 34)), dma((4,)), dma((4,)),
            dma((4, 8)), dma((4, 8)), dma((32,)), dma((32,)), dma((2,)), dma((2,)), dma((13,)),
        ],
        compiler_params=pltpu.CompilerParams(
            collective_id=0, has_side_effects=True, vmem_limit_bytes=60 * 1024 * 1024
        ),
    )(
        feats[0],
        conv_w.transpose(1, 0, 2),
        qkv_w,
        out_w,
        head_w,
        conv_bias,
        head_bias.reshape(8, 128),
        exon_lists[:, 0].transpose(0, 2, 1),
    )


def solution(mesh):
    in_specs = (
        P("win", None, None),
        P("win", None, "mp"),
        P("mp"),
        P("win", "mp"),
        P("win", "mp"),
        P("win", "mp"),
        P("mp"),
        P(None, "win", None, None),
    )
    return jax.shard_map(
        local, mesh=mesh, in_specs=in_specs, out_specs=P(("segment", "win"), "mp"), check_vma=False
    )
```

```python
import math

import jax
import jax.numpy as jnp
from jax import lax
from jax.experimental import pallas as pl
from jax.experimental.pallas import tpu as pltpu
from jax.sharding import PartitionSpec as P

MESH = pl.DeviceIdType.MESH
F32 = jnp.float32
BF16 = jnp.bfloat16

KEY = 64
VAL = 192
TAPS = 5
STEP = 4
BINS = 256
D = 1536
ROWS = 48
COLS = 192
WIDE = 640
TAIL = 384
KV = 256
TRK = 512
NZ = 8
NY = 4

QUICK = (
    ((("O", 0), ("zp", "zm", "xp", "zp2", "zm2", "cp")),),
    (
        (("O", -1), ("cp",)),
        (("O", 1), ("cp",)),
        (("X", 0), ("zp", "zm", "cp")),
        (("O", -2), ("zp", "xp", "cp")),
        (("O", 2), ("zm", "cp")),
    ),
    (
        (("O", -3), ("zp", "xp", "cp")),
        (("O", 3), ("xp", "cp")),
        (("X", 1), ("zm", "cp")),
        (("X", -1), ("cp",)),
        (("X", -2), ("cp",)),
    ),
    (
        (("O", -4), ("xp", "cp")),
        (("X", 2), ("cp",)),
        (("X", 3), ("cp",)),
        (("X", -3), ("cp",)),
    ),
    ((("X", -4), ("cp",)),),
)
LEAN = (
    ((("O", 0), ("zp", "zm", "xp", "cp")),),
    ((("O", -1), ("zp", "cp")), (("O", 1), ("zm", "cp")), (("X", 0), ("zp", "zm", "cp"))),
    (
        (("O", -2), ("zp", "xp", "cp")),
        (("O", 2), ("zm", "cp")),
        (("X", 1), ("zm", "cp")),
        (("X", -1), ("cp",)),
    ),
    (
        (("O", -3), ("zp", "xp", "cp")),
        (("O", 3), ("xp", "cp")),
        (("X", 2), ("cp",)),
        (("X", -2), ("cp",)),
    ),
    ((("O", -4), ("xp", "cp")), (("X", 3), ("cp",)), (("X", -3), ("cp",))),
    ((("X", -4), ("cp",)),),
)


def nt(left, right):
    return lax.dot_general(left, right, (((1,), (1,)), ((), ())), preferred_element_type=F32)


def nn(left, right):
    return lax.dot_general(left, right, (((1,), (0,)), ((), ())), preferred_element_type=F32)


def tn(left, right):
    return lax.dot_general(left, right, (((0,), (0,)), ((), ())), preferred_element_type=F32)


def gelu(x):
    return 0.5 * x * (1.0 + jnp.tanh(math.sqrt(2.0 / math.pi) * (x + 0.044715 * (x * x * x))))


def kernel(
    feats_h, conv_h, qkv_h, outw_h, head_h, cbias_h, hbias_h, exon_h,
    out,
    feats, conv, qkv, cbias, hbias, exon, pa, pb, pk, ph, po,
    wa, wb, wk, wh, wo, wo2, gx, ga, gr, ft, y, wqt, wkt, wht, hcol, trk, gmat, ex_out, ex_in, gs, gin,
    ring_r, ring_s, rsy, ssy, rsa, ssa, rsg, ssg, rse, sse, lsem,
):
    s = lax.axis_index("segment")
    w = lax.axis_index("win")
    m = lax.axis_index("mp")
    h = w // (2 * NZ)
    z = (w // 2) % NZ
    c = w % 2
    b = (s + h) % 2
    q = 2 * m + b

    def win_of(hh, zz, cc):
        return hh * (2 * NZ) + zz * 2 + cc

    where = {
        "zp": {"win": win_of(h, (z + 1) % NZ, c)},
        "zm": {"win": win_of(h, (z + NZ - 1) % NZ, c)},
        "zp2": {"win": win_of(h, (z + 2) % NZ, c)},
        "zm2": {"win": win_of(h, (z + NZ - 2) % NZ, c)},
        "xp": {"segment": 1 - s, "win": win_of(1 - h, z, c)},
        "cp": {"win": win_of(h, z, 1 - c)},
        "sp": {"segment": 1 - s},
        "yp": {"mp": (m + 1) % NY},
        "ym": {"mp": (m + NY - 1) % NY},
        "y2": {"mp": (m + 2) % NY},
    }

    def to(name):
        d = {"segment": s, "win": w, "mp": m}
        d.update(where[name])
        return (d["segment"], d["win"], d["mp"])

    barrier = pltpu.get_barrier_semaphore()
    for name in where:
        pl.semaphore_signal(barrier, inc=1, device_id=to(name), device_id_type=MESH)

    local_copies = [
        pltpu.make_async_copy(src, dst, lsem.at[i])
        for i, (src, dst) in enumerate(
            (
                (conv_h, conv),
                (qkv_h, qkv),
                (feats_h, feats),
                (head_h.at[:, pl.ds(pl.multiple_of(b * TRK, TRK), TRK)], ph),
                (outw_h, po),
                (exon_h, exon),
                (cbias_h, cbias),
                (hbias_h, hbias),
            )
        )
    ]
    for copy in local_copies:
        copy.start()

    def remote(src, dst, send, recv, device):
        return pltpu.make_async_remote_copy(
            src_ref=src, dst_ref=dst, send_sem=send, recv_sem=recv, device_id=device, device_id_type=MESH
        )

    lane = lax.broadcasted_iota(jnp.int32, (1, 128), 1)
    low = lane < 64
    local_copies[0].wait()
    local_copies[1].wait()
    thin = []
    for tap in range(TAPS):
        part = conv[tap].astype(F32)
        part = jnp.where(b == 0, part, pltpu.roll(part, COLS, 1))
        pa[:, tap * 128 : tap * 128 + 128] = part[:, :128].astype(BF16)
        thin.append(part[:, 128:256])
    head_part = qkv[...].astype(F32)
    head_part = jnp.where(b == 0, head_part, pltpu.roll(head_part, 320, 1))
    thin.append(head_part[:, :128])
    for i in range(3):
        pb[:, i * 128 : i * 128 + 128] = jnp.where(low, thin[2 * i], pltpu.roll(thin[2 * i + 1], 64, 1)).astype(BF16)
    pk[...] = pltpu.roll(head_part, 576, 1)[:, :KV].astype(BF16)

    pl.semaphore_wait(barrier, len(where))

    def ring(index, plan, own, buf):
        count = [0]
        tail = []

        def rows(win):
            return buf.at[pl.ds(pl.multiple_of(win * ROWS, ROWS), ROWS), :]

        def shard_win(code, core):
            kind, d = code
            return win_of(h if kind == "O" else 1 - h, (z + d + NZ) % NZ, core)

        def recv(win):
            return ring_r.at[index, win]

        def wait(win):
            remote(rows(win), rows(win), ring_s.at[index, 0], recv(win), to("cp")).wait_recv()

        def step(r):
            for code, names in plan[r]:
                win = shard_win(code, c)
                src = rows(win)
                if code == ("O", 0):
                    src = rows(win) if own is None else own
                else:
                    wait(win)
                for name in names:
                    copy = remote(src, rows(win), ring_s.at[index, count[0]], recv(win), to(name))
                    count[0] += 1
                    copy.start()
                    tail.append(copy)

        def rest():
            for group in plan:
                for code, names in group:
                    wait(shard_win(code, 1 - c))

        def flush():
            for copy in tail:
                copy.wait_send()

        keep = None
        if own is not None:
            keep = pltpu.make_async_copy(own, rows(w), lsem.at[8 + index])
        return step, rest, flush, keep

    def gather(buf, index, lo, n):
        def rows(dm, other, skip=0, count=n):
            slot = 2 * ((m + dm + NY) % NY) + (1 - b if other else b)
            return buf.at[pl.ds(pl.multiple_of(slot * COLS + lo + skip, 16), count), :]

        half = n // 2
        tail = []

        def push(i, ref, name):
            copy = remote(ref, ref, ssa.at[index, i], rsa.at[index, i], to(name))
            copy.start()
            tail.append(copy)

        def got(i, ref):
            remote(ref, ref, ssa.at[index, i], rsa.at[index, i], to("sp")).wait_recv()

        def start():
            own = rows(0, False)
            push(0, own, "yp")
            push(1, own, "ym")
            push(2, own, "sp")

        def first():
            got(0, rows(-1, False))
            push(3, rows(-1, False, 0, half), "yp")
            got(1, rows(1, False))
            push(4, rows(1, False, half, half), "ym")
            got(2, rows(0, True))
            push(5, rows(0, True), "yp")
            push(6, rows(0, True), "ym")

        def second():
            got(3, rows(2, False, 0, half))
            got(4, rows(2, False, half, half))
            push(7, rows(2, False), "sp")

        def third():
            got(5, rows(-1, True))
            got(6, rows(1, True))
            got(7, rows(2, True))

        def flush():
            for copy in tail:
                copy.wait_send()

        return start, first, second, third, flush

    step_a, rest_a, flush_a, keep_a = ring(0, QUICK, pa, wa)
    step_b, rest_b, flush_b, keep_b = ring(1, QUICK, pb, wb)
    step_k, rest_k, flush_k, keep_k = ring(2, LEAN, pk, wk)
    step_h, rest_h, flush_h, keep_h = ring(3, LEAN, ph, wh)
    step_o, rest_o, flush_o, _ = ring(4, LEAN, None, wo)
    step_p, rest_p, flush_p, _ = ring(5, LEAN, None, wo2)

    start_x, first_x, second_x, third_x, flush_x = gather(gx, 0, 0, 128)
    start_u, first_u, second_u, third_u, flush_u = gather(gx, 1, 128, 64)
    start_v, first_v, second_v, third_v, flush_v = gather(ga, 2, 0, 96)
    start_w, first_w, second_w, third_w, flush_w = gather(ga, 3, 96, 96)

    step_a(0)
    step_b(0)
    step_k(0)
    keep_a.start()
    keep_b.start()
    keep_k.start()

    def wo_part(buf, model):
        return buf.at[
            pl.ds(pl.multiple_of(w * ROWS, ROWS), ROWS),
            pl.ds(pl.multiple_of((model % 2) * 2 * COLS, 2 * COLS), 2 * COLS),
        ]

    for i in range(2, len(local_copies)):
        local_copies[i].wait()
    keep_h.start()

    def each_part(model, act):
        @pl.when(model < 2)
        def _():
            act(wo_part(wo, model))

        @pl.when(model >= 2)
        def _():
            act(wo_part(wo2, model))

    hops = (("yp", 1), ("ym", 3), ("y2", 2))
    each_part(m, lambda ref: pltpu.make_async_copy(po, ref, lsem.at[12]).start())
    for name, j in hops:
        each_part(m, lambda ref, name=name, j=j: remote(po, ref, ssy.at[j], rsy.at[j], to(name)).start())

    def wo_ready():
        each_part(m, lambda ref: pltpu.make_async_copy(po, ref, lsem.at[12]).wait())
        for name, j in hops:
            each_part(
                (m - j + NY) % NY, lambda ref, j=j: remote(po, ref, ssy.at[j], rsy.at[j], to("cp")).wait_recv()
            )

    eye = (
        lax.broadcasted_iota(jnp.int32, (BINS, BINS), 0) == lax.broadcasted_iota(jnp.int32, (BINS, BINS), 1)
    ).astype(F32).astype(BF16)

    @pl.loop(0, D // BINS)
    def _(n):
        at = pl.ds(pl.multiple_of(n * BINS, BINS), BINS)
        ft[:, at] = nt(eye, feats[at, :]).astype(BF16)

    step_a(1)
    step_b(1)
    step_h(0)

    rows_id = lax.broadcasted_iota(jnp.int32, (512, 64), 0)
    owner = (
        ((rows_id // 128) % 2) * 32 + ((rows_id // 64) % 2) * 16 + ((rows_id // 8) % 8) * 2 + rows_id // 256
    )
    repeat = (owner == lax.broadcasted_iota(jnp.int32, (512, 64), 1)).astype(F32).astype(BF16)
    first_bin = nt(repeat, exon[0].astype(F32).astype(BF16))
    end_bin = nt(repeat, exon[1].astype(F32).astype(BF16))
    gene = nt(repeat, exon[2].astype(F32).astype(BF16))

    def gene_bins(blk):
        at = slice(blk * 64, blk * 64 + 64)
        bins = lax.broadcasted_iota(jnp.int32, (64, BINS), 1).astype(F32)
        which = (lax.broadcasted_iota(jnp.int32, (64, 1), 0) % 8).astype(F32)
        total = jnp.zeros((64, BINS), F32)
        for j in range(8):
            lo = jnp.where(gene[at, j : j + 1] == which, first_bin[at, j : j + 1], 1024.0)
            inside = jnp.logical_and(bins >= lo, bins < end_bin[at, j : j + 1])
            total = total + jnp.where(inside, 1.0, 0.0)
        gmat[at, :] = total.astype(BF16)

    for blk in range(2):
        gene_bins(blk)
    step_a(2)
    step_b(2)
    step_k(1)
    step_h(1)
    step_a(3)
    step_b(3)
    step_k(2)
    wo_ready()
    step_o(0)
    step_p(0)
    step_a(4)
    step_h(2)
    step_b(4)
    keep_a.wait()
    rest_a()

    t_row = lax.broadcasted_iota(jnp.int32, (BINS, 128), 0)

    def shifted(x, tap):
        by = (tap - TAPS // 2) * STEP
        if by == 0:
            return x
        moved = pltpu.roll(x, (BINS - by) % BINS, 0)
        ok = jnp.logical_and(t_row + by >= 0, t_row + by < BINS)
        return jnp.where(ok, moved, 0.0)

    c0, c1, c2 = (cbias[i * 128 : i * 128 + 128].reshape(1, 128) for i in range(3))
    wide_bias = jnp.where(b == 0, c0, pltpu.roll(jnp.where(low, c2, c1), 64, 1))
    narrow_bias = jnp.where(b == 0, c1, pltpu.roll(c2, 64, 1))
    base = pl.multiple_of(q * COLS, COLS)
    base2 = pl.multiple_of(q * COLS + 128, 64)

    for i in range(TAPS):
        y[:, i * 128 : i * 128 + 128] = nn(ft[...], wa[:, i * 128 : i * 128 + 128])
    wide = shifted(y[:, 0:128], 0)
    for tap in range(1, TAPS):
        wide = wide + shifted(y[:, tap * 128 : tap * 128 + 128], tap)
    wide = gelu(wide + wide_bias).T
    gx[pl.ds(base, 128), :] = (feats[pl.ds(base, 128), :].astype(F32) + wide).astype(BF16)
    start_x()

    keep_b.wait()
    rest_b()
    step_o(1)
    pairs = [nn(ft[...], wb[:, i * 128 : i * 128 + 128]) for i in range(3)]
    even = shifted(pairs[0], 0) + shifted(pairs[1], 2) + shifted(pairs[2], 4)
    odd = shifted(pairs[0], 1) + shifted(pairs[1], 3)
    narrow = even + pltpu.roll(odd, 64, 1)
    narrow = gelu(narrow + narrow_bias).T
    gx[pl.ds(base2, 64), :] = (feats[pl.ds(base2, 64), :].astype(F32) + narrow[:64]).astype(BF16)
    start_u()
    step_k(3)
    step_p(1)
    first_x()
    step_h(3)
    for blk in range(2, 4):
        gene_bins(blk)
    first_u()
    step_o(2)
    wqt[...] = nt(eye[:128, :128], wb[:, 256:384]).astype(BF16)
    second_x()
    step_k(4)
    second_u()
    step_p(2)
    third_x()
    step_k(5)
    step_o(3)
    third_u()
    keep_k.wait()
    rest_k()
    wkt[...] = nt(eye, wk[...]).astype(BF16)

    qq = nn(wqt[...], gx[...])[64:128].astype(BF16)
    kv = nn(wkt[...], gx[...]).astype(BF16)
    scores = tn(kv[0:64], qq) * (1.0 / math.sqrt(KEY))
    weights = jnp.exp(scores)
    prob = (weights / jnp.sum(weights, axis=0, keepdims=True)).astype(BF16)
    ga[pl.ds(base, COLS), :] = nn(kv[64:256], prob).astype(BF16)

    start_v()
    step_h(4)
    step_p(3)
    start_w()
    for blk in range(4, 6):
        gene_bins(blk)
    first_v()
    step_h(5)
    step_o(4)
    first_w()
    keep_h.wait()
    rest_h()
    step_p(4)
    for blk in range(6, 8):
        gene_bins(blk)
    second_v()
    step_o(5)
    second_w()
    for i in range(TRK // 256):
        wht[i * 256 : i * 256 + 256, :] = nt(eye, wh[:, i * 256 : i * 256 + 256]).astype(BF16)
    eye_f = (
        lax.broadcasted_iota(jnp.int32, (128, 128), 0) == lax.broadcasted_iota(jnp.int32, (128, 128), 1)
    )
    for i in range(TRK // 128):
        row = jnp.where(b == 0, hbias[i : i + 1, :], hbias[4 + i : 5 + i, :])
        hcol[i * 128 : i * 128 + 128, :] = jnp.sum(jnp.where(eye_f, row, 0.0), axis=1, keepdims=True)
    step_p(5)
    flush_a()
    flush_b()
    third_v()
    third_w()
    rest_o()
    rest_p()

    for i in range(D // 256):
        at = slice(i * 256, i * 256 + 256)
        gr[at, :] = (gx[at, :].astype(F32) + (nn(wo[at, :], ga[0 : D // 2, :]) + nn(wo2[at, :], ga[D // 2 :, :]))).astype(BF16)

    def sums(core, blk):
        rows = gmat[pl.ds(pl.multiple_of(core * 256, 256), 256), :]
        return nt(rows, trk[blk * 256 : blk * 256 + 256, :]).reshape(32, 8, 256)

    swaps = []
    for blk in range(TRK // 256):
        at = slice(blk * 256, blk * 256 + 256)
        logits = nn(wht[at, :], gr[...]) + hcol[at, :]
        soft = jnp.maximum(logits, 0.0) + jnp.log1p(jnp.exp(-jnp.abs(logits)))
        trk[at, :] = soft.astype(BF16)
        give = sums(1 - c, blk)
        ex_out[blk] = jnp.concatenate([give[:, :, :128], give[:, :, 128:]], axis=1).astype(BF16)
        swaps.append(remote(ex_out.at[blk], ex_in.at[blk], sse.at[blk], rse.at[blk], to("cp")))
        swaps[blk].start()
    keep_sums = [sums(c, blk) for blk in range(TRK // 256)]
    for blk in range(TRK // 256):
        swaps[blk].wait_recv()
        took = ex_in[blk].astype(F32)
        keep_sums[blk] = keep_sums[blk] + jnp.concatenate([took[:, :8], took[:, 8:]], axis=2)
    gs[...] = jnp.concatenate(keep_sums, axis=1).astype(BF16)

    def gene_copy(rel):
        ds, dh, dz = rel // 16, (rel // 8) % 2, rel % 8
        s2, h2, z2 = (s + ds) % 2, (h + dh) % 2, (z + dz) % NZ
        return remote(
            gs.at[s2 * 16 + h2 * 8 + z2],
            gin.at[rel],
            ssg.at[rel],
            rsg.at[rel],
            (s2, win_of(h2, z2, c), m),
        )

    gene_copies = [gene_copy(part * 8 + dz) for dz in (4, 3, 5, 2, 6, 1, 7, 0) for part in (3, 2, 1, 0) if part + dz]
    for copy in gene_copies:
        copy.start()

    gin[0] = gs[s * 16 + h * 8 + z]
    flush_k()
    flush_h()
    flush_o()
    flush_p()
    flush_x()
    flush_u()
    flush_v()
    flush_w()
    for name, j in hops:
        each_part(m, lambda ref, name=name, j=j: remote(po, ref, ssy.at[j], rsy.at[j], to(name)).wait_send())
    for swap in swaps:
        swap.wait_send()
    for copy in gene_copies:
        copy.wait()

    same = gin[0].astype(F32)
    other = gin[8].astype(F32)
    for rel in range(1, 8):
        same = same + gin[rel].astype(F32)
        other = other + gin[8 + rel].astype(F32)
    for rel in range(8):
        other = other + gin[16 + rel].astype(F32)
        same = same + gin[24 + rel].astype(F32)
    for value, at in ((same, b), (other, 1 - b)):
        value = jnp.log1p(value)
        out[:, pl.ds(pl.multiple_of(at * TRK, TRK), 256)] = value[0:8]
        out[:, pl.ds(pl.multiple_of(at * TRK + 256, 256), 256)] = value[8:16]


def local(feats, conv_w, conv_bias, qkv_w, out_w, head_w, head_bias, exon_lists):
    vmem = pltpu.VMEM
    dma = pltpu.SemaphoreType.DMA
    anywhere = pl.BlockSpec(memory_space=pltpu.HBM)
    return pl.pallas_call(
        kernel,
        out_shape=jax.ShapeDtypeStruct((8, 1024), F32),
        in_specs=[anywhere] * 8,
        out_specs=pl.BlockSpec(memory_space=pltpu.VMEM),
        scratch_shapes=[
            vmem((D, BINS), BF16),
            vmem((TAPS, ROWS, 2 * COLS), BF16),
            vmem((ROWS, 640), BF16),
            vmem((384,), F32),
            vmem((8, 128), F32),
            vmem((3, 8, 64), jnp.int32),
            vmem((ROWS, WIDE), BF16),
            vmem((ROWS, TAIL), BF16),
            vmem((ROWS, KV), BF16),
            vmem((ROWS, TRK), BF16),
            vmem((ROWS, 2 * COLS), BF16),
            vmem((D, WIDE), BF16),
            vmem((D, TAIL), BF16),
            vmem((D, KV), BF16),
            vmem((D, TRK), BF16),
            vmem((D, D // 2), BF16),
            vmem((D, D // 2), BF16),
            vmem((D, BINS), BF16),
            vmem((D, BINS), BF16),
            vmem((D, BINS), BF16),
            vmem((BINS, D), BF16),
            vmem((BINS, WIDE), F32),
            vmem((128, D), BF16),
            vmem((KV, D), BF16),
            vmem((TRK, D), BF16),
            vmem((TRK, 1), F32),
            vmem((TRK, BINS), BF16),
            vmem((512, BINS), BF16),
            vmem((2, 32, 16, 128), BF16),
            vmem((2, 32, 16, 128), BF16),
            vmem((32, 16, 256), BF16),
            vmem((32, 16, 256), BF16),
            dma((6, 32)), dma((6, 34)), dma((4,)), dma((4,)),
            dma((4, 8)), dma((4, 8)), dma((32,)), dma((32,)), dma((2,)), dma((2,)), dma((13,)),
        ],
        compiler_params=pltpu.CompilerParams(
            collective_id=0, has_side_effects=True, vmem_limit_bytes=60 * 1024 * 1024
        ),
    )(
        feats[0],
        conv_w.transpose(1, 0, 2),
        qkv_w,
        out_w,
        head_w,
        conv_bias,
        head_bias.reshape(8, 128),
        exon_lists[:, 0].transpose(0, 2, 1),
    )


def solution(mesh):
    in_specs = (
        P("win", None, None),
        P("win", None, "mp"),
        P("mp"),
        P("win", "mp"),
        P("win", "mp"),
        P("win", "mp"),
        P("mp"),
        P(None, "win", None, None),
    )
    return jax.shard_map(
        local, mesh=mesh, in_specs=in_specs, out_specs=P(("segment", "win"), "mp"), check_vma=False
    )
```

```python
import math

import jax
import jax.numpy as jnp
from jax import lax
from jax.experimental import pallas as pl
from jax.experimental.pallas import tpu as pltpu
from jax.sharding import PartitionSpec as P

MESH = pl.DeviceIdType.MESH
F32 = jnp.float32
BF16 = jnp.bfloat16

KEY = 64
VAL = 192
TAPS = 5
STEP = 4
BINS = 256
D = 1536
ROWS = 48
COLS = 192
WIDE = 384
WIDE2 = 256
TAIL = 384
KV = 256
TRK = 512
NZ = 8
NY = 4

TREE = {
    ("O", 0): ("zp2", "zm2", "xp"),
    ("X", 0): ("zm",),
    ("O", -2): ("xp", "zm", "zp"),
    ("O", 2): ("zm", "xp", "zp"),
    ("X", 1): (),
    ("X", -2): ("zp2",),
    ("O", -3): ("xp",),
    ("O", -1): ("xp",),
    ("X", 2): ("zm",),
    ("O", 1): (),
    ("O", 3): ("zm",),
    ("X", -3): (),
    ("X", 3): (),
    ("X", -1): (),
    ("O", -4): (),
    ("X", -4): (),
}
EARLY = (
    (0, "O", 0), (1, "O", 0), (2, "O", 0), (0, "X", 0), (1, "X", 0), (2, "X", 0), (0, "O", -2), (0, "O", 2),
    (1, "O", -2), (1, "O", 2), (2, "O", -2), (2, "O", 2), (0, "X", 1), (1, "X", 1), (2, "X", 1), (0, "X", -2),
    (0, "O", -3), (0, "O", -1), (0, "X", 2), (0, "O", 1), (1, "X", -2), (0, "O", 3), (1, "O", -3), (1, "X", 2),
    (1, "O", -1), (1, "O", 1), (1, "O", 3), (2, "X", -2), (2, "O", -3), (2, "O", -1), (2, "X", 2), (2, "O", 1),
    (2, "O", 3), (0, "X", -3), (0, "X", 3), (0, "X", -1), (1, "X", -3), (0, "O", -4), (0, "X", -4), (1, "X", -1),
    (1, "X", 3), (1, "O", -4), (1, "X", -4), (2, "X", -3), (2, "X", 3), (2, "X", -1), (2, "O", -4), (2, "X", -4),
)
LEAN = (
    ((("O", 0), ("zp", "zm", "xp", "cp")),),
    ((("O", -1), ("zp", "cp")), (("O", 1), ("zm", "cp")), (("X", 0), ("zp", "zm", "cp"))),
    (
        (("O", -2), ("zp", "xp", "cp")),
        (("O", 2), ("zm", "cp")),
        (("X", 1), ("zm", "cp")),
        (("X", -1), ("cp",)),
    ),
    (
        (("O", -3), ("zp", "xp", "cp")),
        (("O", 3), ("xp", "cp")),
        (("X", 2), ("cp",)),
        (("X", -2), ("cp",)),
    ),
    ((("O", -4), ("xp", "cp")), (("X", 3), ("cp",)), (("X", -3), ("cp",))),
    ((("X", -4), ("cp",)),),
)


def nt(left, right):
    return lax.dot_general(left, right, (((1,), (1,)), ((), ())), preferred_element_type=F32)


def nn(left, right):
    return lax.dot_general(left, right, (((1,), (0,)), ((), ())), preferred_element_type=F32)


def tn(left, right):
    return lax.dot_general(left, right, (((0,), (0,)), ((), ())), preferred_element_type=F32)


def gelu(x):
    return 0.5 * x * (1.0 + jnp.tanh(math.sqrt(2.0 / math.pi) * (x + 0.044715 * (x * x * x))))


def kernel(
    feats_h, conv_h, qkv_h, outw_h, head_h, cbias_h, hbias_h, exon_h,
    out,
    feats, conv, qkv, cbias, hbias, exon, pa, pa2, pb, pk, ph, po,
    wa, wa2, wb, wk, wh, wo, wo2, gx, ga, gr, ft, y, wqt, wkt, wht, hcol, trk, gmat, ex_out, ex_in, gs, gin,
    ring_r, ring_s, rsy, ssy, rsa, ssa, rsg, ssg, rse, sse, lsem,
):
    s = lax.axis_index("segment")
    w = lax.axis_index("win")
    m = lax.axis_index("mp")
    h = w // (2 * NZ)
    z = (w // 2) % NZ
    c = w % 2
    b = (s + h) % 2
    q = 2 * m + b

    def win_of(hh, zz, cc):
        return hh * (2 * NZ) + zz * 2 + cc

    where = {
        "zp": {"win": win_of(h, (z + 1) % NZ, c)},
        "zm": {"win": win_of(h, (z + NZ - 1) % NZ, c)},
        "zp2": {"win": win_of(h, (z + 2) % NZ, c)},
        "zm2": {"win": win_of(h, (z + NZ - 2) % NZ, c)},
        "xp": {"segment": 1 - s, "win": win_of(1 - h, z, c)},
        "cp": {"win": win_of(h, z, 1 - c)},
        "sp": {"segment": 1 - s},
        "yp": {"mp": (m + 1) % NY},
        "ym": {"mp": (m + NY - 1) % NY},
        "y2": {"mp": (m + 2) % NY},
    }

    def to(name):
        d = {"segment": s, "win": w, "mp": m}
        d.update(where[name])
        return (d["segment"], d["win"], d["mp"])

    barrier = pltpu.get_barrier_semaphore()
    for name in where:
        pl.semaphore_signal(barrier, inc=1, device_id=to(name), device_id_type=MESH)

    local_copies = [
        pltpu.make_async_copy(src, dst, lsem.at[i])
        for i, (src, dst) in enumerate(
            (
                (conv_h, conv),
                (qkv_h, qkv),
                (feats_h, feats),
                (head_h.at[:, pl.ds(pl.multiple_of(b * TRK, TRK), TRK)], ph),
                (outw_h, po),
                (exon_h, exon),
                (cbias_h, cbias),
                (hbias_h, hbias),
            )
        )
    ]
    for copy in local_copies:
        copy.start()

    def remote(src, dst, send, recv, device):
        return pltpu.make_async_remote_copy(
            src_ref=src, dst_ref=dst, send_sem=send, recv_sem=recv, device_id=device, device_id_type=MESH
        )

    lane = lax.broadcasted_iota(jnp.int32, (1, 128), 1)
    low = lane < 64
    local_copies[0].wait()
    local_copies[1].wait()
    thin = []
    for tap in range(TAPS):
        part = conv[tap].astype(F32)
        part = jnp.where(b == 0, part, pltpu.roll(part, COLS, 1))
        if tap < 3:
            pa[:, tap * 128 : tap * 128 + 128] = part[:, :128].astype(BF16)
        else:
            pa2[:, tap * 128 - 384 : tap * 128 - 256] = part[:, :128].astype(BF16)
        thin.append(part[:, 128:256])
    head_part = qkv[...].astype(F32)
    head_part = jnp.where(b == 0, head_part, pltpu.roll(head_part, 320, 1))
    thin.append(head_part[:, :128])
    for i in range(3):
        pb[:, i * 128 : i * 128 + 128] = jnp.where(low, thin[2 * i], pltpu.roll(thin[2 * i + 1], 64, 1)).astype(BF16)
    pk[...] = pltpu.roll(head_part, 576, 1)[:, :KV].astype(BF16)

    pl.semaphore_wait(barrier, len(where))

    def ring(index, plan, own, buf):
        count = [0]
        tail = []

        def rows(win):
            return buf.at[pl.ds(pl.multiple_of(win * ROWS, ROWS), ROWS), :]

        def shard_win(code, core):
            kind, d = code
            return win_of(h if kind == "O" else 1 - h, (z + d + NZ) % NZ, core)

        def recv(win):
            return ring_r.at[index, win]

        def wait(win):
            remote(rows(win), rows(win), ring_s.at[index, 0], recv(win), to("cp")).wait_recv()

        def take(code, names):
            win = shard_win(code, c)
            src = rows(win)
            if code == ("O", 0):
                src = rows(win) if own is None else own
            else:
                wait(win)
            for name in names:
                copy = remote(src, rows(win), ring_s.at[index, count[0]], recv(win), to(name))
                count[0] += 1
                copy.start()
                tail.append(copy)

        def step(r):
            if plan is None:
                take(r, TREE[r] + ("cp",))
            else:
                for code, names in plan[r]:
                    take(code, names)

        def rest():
            for code in TREE:
                wait(shard_win(code, 1 - c))

        def flush():
            for copy in tail:
                copy.wait_send()

        keep = None
        if own is not None:
            keep = pltpu.make_async_copy(own, rows(w), lsem.at[13 + index])
        return step, rest, flush, keep

    def gather(buf, index, lo, n):
        def rows(dm, other, skip=0, count=n):
            slot = 2 * ((m + dm + NY) % NY) + (1 - b if other else b)
            return buf.at[pl.ds(pl.multiple_of(slot * COLS + lo + skip, 16), count), :]

        half = n // 2
        tail = []

        def push(i, ref, name):
            copy = remote(ref, ref, ssa.at[index, i], rsa.at[index, i], to(name))
            copy.start()
            tail.append(copy)

        def got(i, ref):
            remote(ref, ref, ssa.at[index, i], rsa.at[index, i], to("sp")).wait_recv()

        def start():
            own = rows(0, False)
            push(0, own, "yp")
            push(1, own, "ym")
            push(2, own, "sp")

        def first():
            got(0, rows(-1, False))
            push(3, rows(-1, False, 0, half), "yp")
            got(1, rows(1, False))
            push(4, rows(1, False, half, half), "ym")
            got(2, rows(0, True))
            push(5, rows(0, True), "yp")
            push(6, rows(0, True), "ym")

        def second():
            got(3, rows(2, False, 0, half))
            got(4, rows(2, False, half, half))
            push(7, rows(2, False), "sp")

        def third():
            got(5, rows(-1, True))
            got(6, rows(1, True))
            got(7, rows(2, True))

        def flush():
            for copy in tail:
                copy.wait_send()

        return start, first, second, third, flush

    step_a, rest_a, flush_a, keep_a = ring(0, None, pa, wa)
    step_a2, rest_a2, flush_a2, keep_a2 = ring(6, None, pa2, wa2)
    step_b, rest_b, flush_b, keep_b = ring(1, None, pb, wb)
    step_k, rest_k, flush_k, keep_k = ring(2, LEAN, pk, wk)
    step_h, rest_h, flush_h, keep_h = ring(3, LEAN, ph, wh)
    step_o, rest_o, flush_o, _ = ring(4, LEAN, None, wo)
    step_p, rest_p, flush_p, _ = ring(5, LEAN, None, wo2)

    start_x, first_x, second_x, third_x, flush_x = gather(gx, 0, 0, 128)
    start_u, first_u, second_u, third_u, flush_u = gather(gx, 1, 128, 64)
    start_v, first_v, second_v, third_v, flush_v = gather(ga, 2, 0, 96)
    start_w, first_w, second_w, third_w, flush_w = gather(ga, 3, 96, 96)

    early_steps = (step_a, step_a2, step_b)

    def early(first, last):
        for stream, kind, d in EARLY[first:last]:
            early_steps[stream]((kind, d))

    early(0, 3)
    keep_a.start()
    keep_a2.start()
    keep_b.start()
    keep_k.start()

    def wo_part(buf, model):
        return buf.at[
            pl.ds(pl.multiple_of(w * ROWS, ROWS), ROWS),
            pl.ds(pl.multiple_of((model % 2) * 2 * COLS, 2 * COLS), 2 * COLS),
        ]

    for i in range(2, len(local_copies)):
        local_copies[i].wait()
    keep_h.start()

    def each_part(model, act):
        @pl.when(model < 2)
        def _():
            act(wo_part(wo, model))

        @pl.when(model >= 2)
        def _():
            act(wo_part(wo2, model))

    hops = (("yp", 1), ("ym", 3), ("y2", 2))
    each_part(m, lambda ref: pltpu.make_async_copy(po, ref, lsem.at[12]).start())
    for name, j in hops:
        each_part(m, lambda ref, name=name, j=j: remote(po, ref, ssy.at[j], rsy.at[j], to(name)).start())

    def wo_ready():
        each_part(m, lambda ref: pltpu.make_async_copy(po, ref, lsem.at[12]).wait())
        for name, j in hops:
            each_part(
                (m - j + NY) % NY, lambda ref, j=j: remote(po, ref, ssy.at[j], rsy.at[j], to("cp")).wait_recv()
            )

    eye = (
        lax.broadcasted_iota(jnp.int32, (BINS, BINS), 0) == lax.broadcasted_iota(jnp.int32, (BINS, BINS), 1)
    ).astype(F32).astype(BF16)

    early(3, 9)

    rows_id = lax.broadcasted_iota(jnp.int32, (512, 64), 0)
    owner = (
        ((rows_id // 128) % 2) * 32 + ((rows_id // 64) % 2) * 16 + ((rows_id // 8) % 8) * 2 + rows_id // 256
    )
    repeat = (owner == lax.broadcasted_iota(jnp.int32, (512, 64), 1)).astype(F32).astype(BF16)
    first_bin = nt(repeat, exon[0].astype(F32).astype(BF16))
    end_bin = nt(repeat, exon[1].astype(F32).astype(BF16))
    gene = nt(repeat, exon[2].astype(F32).astype(BF16))

    def gene_bins(blk):
        at = slice(blk * 64, blk * 64 + 64)
        bins = lax.broadcasted_iota(jnp.int32, (64, BINS), 1).astype(F32)
        which = (lax.broadcasted_iota(jnp.int32, (64, 1), 0) % 8).astype(F32)
        total = jnp.zeros((64, BINS), F32)
        for j in range(8):
            lo = jnp.where(gene[at, j : j + 1] == which, first_bin[at, j : j + 1], 1024.0)
            inside = jnp.logical_and(bins >= lo, bins < end_bin[at, j : j + 1])
            total = total + jnp.where(inside, 1.0, 0.0)
        gmat[at, :] = total.astype(BF16)

    gene_bins(0)
    early(9, 14)
    step_k(0)
    early(14, 17)
    gene_bins(1)
    early(17, 25)
    wo_ready()
    step_o(0)

    @pl.loop(0, D // BINS)
    def _(n):
        at = pl.ds(pl.multiple_of(n * BINS, BINS), BINS)
        ft[:, at] = nt(eye, feats[at, :]).astype(BF16)

    early(25, 31)
    step_k(1)
    early(31, 39)
    step_p(0)
    early(39, 40)
    for blk in range(2, 4):
        gene_bins(blk)
    early(40, 43)
    step_h(0)
    early(43, 45)
    step_o(1)
    early(45, 46)
    step_k(2)
    early(46, 48)
    keep_a.wait()
    keep_a2.wait()
    rest_a()
    rest_a2()

    t_row = lax.broadcasted_iota(jnp.int32, (BINS, 128), 0)

    def shifted(x, tap):
        by = (tap - TAPS // 2) * STEP
        if by == 0:
            return x
        moved = pltpu.roll(x, (BINS - by) % BINS, 0)
        ok = jnp.logical_and(t_row + by >= 0, t_row + by < BINS)
        return jnp.where(ok, moved, 0.0)

    c0, c1, c2 = (cbias[i * 128 : i * 128 + 128].reshape(1, 128) for i in range(3))
    wide_bias = jnp.where(b == 0, c0, pltpu.roll(jnp.where(low, c2, c1), 64, 1))
    narrow_bias = jnp.where(b == 0, c1, pltpu.roll(c2, 64, 1))
    base = pl.multiple_of(q * COLS, COLS)
    base2 = pl.multiple_of(q * COLS + 128, 64)

    for i in range(TAPS):
        part = wa[:, i * 128 : i * 128 + 128] if i < 3 else wa2[:, i * 128 - 384 : i * 128 - 256]
        y[:, i * 128 : i * 128 + 128] = nn(ft[...], part)
    wide = shifted(y[:, 0:128], 0)
    for tap in range(1, TAPS):
        wide = wide + shifted(y[:, tap * 128 : tap * 128 + 128], tap)
    wide = gelu(wide + wide_bias).T
    gx[pl.ds(base, 128), :] = (feats[pl.ds(base, 128), :].astype(F32) + wide).astype(BF16)
    start_x()
    step_h(1)

    keep_b.wait()
    rest_b()
    pairs = [nn(ft[...], wb[:, i * 128 : i * 128 + 128]) for i in range(3)]
    even = shifted(pairs[0], 0) + shifted(pairs[1], 2) + shifted(pairs[2], 4)
    odd = shifted(pairs[0], 1) + shifted(pairs[1], 3)
    narrow = even + pltpu.roll(odd, 64, 1)
    narrow = gelu(narrow + narrow_bias).T
    gx[pl.ds(base2, 64), :] = (feats[pl.ds(base2, 64), :].astype(F32) + narrow[:64]).astype(BF16)
    start_u()
    step_o(2)
    first_x()
    step_k(3)
    step_p(1)
    first_u()
    step_h(2)
    wqt[...] = nt(eye[:128, :128], wb[:, 256:384]).astype(BF16)
    second_x()
    step_k(4)
    second_u()
    step_o(3)
    step_p(2)
    third_x()
    step_k(5)
    step_h(3)
    third_u()
    keep_k.wait()
    rest_k()
    wkt[...] = nt(eye, wk[...]).astype(BF16)

    qq = nn(wqt[...], gx[...])[64:128].astype(BF16)
    kv = nn(wkt[...], gx[...]).astype(BF16)
    scores = tn(kv[0:64], qq) * (1.0 / math.sqrt(KEY))
    weights = jnp.exp(scores)
    prob = (weights / jnp.sum(weights, axis=0, keepdims=True)).astype(BF16)
    ga[pl.ds(base, COLS), :] = nn(kv[64:256], prob).astype(BF16)

    start_v()
    start_w()
    step_o(4)
    step_p(3)
    for blk in range(4, 6):
        gene_bins(blk)
    first_v()
    first_w()
    step_h(4)
    for blk in range(6, 8):
        gene_bins(blk)
    second_v()
    step_o(5)
    step_p(4)
    second_w()
    step_h(5)
    keep_h.wait()
    rest_h()
    for i in range(TRK // 256):
        wht[i * 256 : i * 256 + 256, :] = nt(eye, wh[:, i * 256 : i * 256 + 256]).astype(BF16)
    eye_f = (
        lax.broadcasted_iota(jnp.int32, (128, 128), 0) == lax.broadcasted_iota(jnp.int32, (128, 128), 1)
    )
    for i in range(TRK // 128):
        row = jnp.where(b == 0, hbias[i : i + 1, :], hbias[4 + i : 5 + i, :])
        hcol[i * 128 : i * 128 + 128, :] = jnp.sum(jnp.where(eye_f, row, 0.0), axis=1, keepdims=True)
    step_p(5)
    flush_a()
    flush_a2()
    flush_b()
    third_v()
    third_w()
    rest_o()
    rest_p()

    for i in range(D // 256):
        at = slice(i * 256, i * 256 + 256)
        gr[at, :] = (gx[at, :].astype(F32) + (nn(wo[at, :], ga[0 : D // 2, :]) + nn(wo2[at, :], ga[D // 2 :, :]))).astype(BF16)

    def sums(core, blk):
        rows = gmat[pl.ds(pl.multiple_of(core * 256, 256), 256), :]
        return nt(rows, trk[blk * 256 : blk * 256 + 256, :]).reshape(32, 8, 256)

    swaps = []
    for blk in range(TRK // 256):
        at = slice(blk * 256, blk * 256 + 256)
        logits = nn(wht[at, :], gr[...]) + hcol[at, :]
        soft = jnp.maximum(logits, 0.0) + jnp.log1p(jnp.exp(-jnp.abs(logits)))
        trk[at, :] = soft.astype(BF16)
        give = sums(1 - c, blk)
        ex_out[blk] = jnp.concatenate([give[:, :, :128], give[:, :, 128:]], axis=1).astype(BF16)
        swaps.append(remote(ex_out.at[blk], ex_in.at[blk], sse.at[blk], rse.at[blk], to("cp")))
        swaps[blk].start()
    keep_sums = [sums(c, blk) for blk in range(TRK // 256)]
    for blk in range(TRK // 256):
        swaps[blk].wait_recv()
        took = ex_in[blk].astype(F32)
        keep_sums[blk] = keep_sums[blk] + jnp.concatenate([took[:, :8], took[:, 8:]], axis=2)
    gs[...] = jnp.concatenate(keep_sums, axis=1).astype(BF16)

    def gene_copy(rel):
        ds, dh, dz = rel // 16, (rel // 8) % 2, rel % 8
        s2, h2, z2 = (s + ds) % 2, (h + dh) % 2, (z + dz) % NZ
        return remote(
            gs.at[s2 * 16 + h2 * 8 + z2],
            gin.at[rel],
            ssg.at[rel],
            rsg.at[rel],
            (s2, win_of(h2, z2, c), m),
        )

    gene_copies = [gene_copy(part * 8 + dz) for dz in (4, 3, 5, 2, 6, 1, 7, 0) for part in (3, 2, 1, 0) if part + dz]
    for copy in gene_copies:
        copy.start()

    gin[0] = gs[s * 16 + h * 8 + z]
    flush_k()
    flush_h()
    flush_o()
    flush_p()
    flush_x()
    flush_u()
    flush_v()
    flush_w()
    for name, j in hops:
        each_part(m, lambda ref, name=name, j=j: remote(po, ref, ssy.at[j], rsy.at[j], to(name)).wait_send())
    for swap in swaps:
        swap.wait_send()
    for copy in gene_copies:
        copy.wait()

    same = gin[0].astype(F32)
    other = gin[8].astype(F32)
    for rel in range(1, 8):
        same = same + gin[rel].astype(F32)
        other = other + gin[8 + rel].astype(F32)
    for rel in range(8):
        other = other + gin[16 + rel].astype(F32)
        same = same + gin[24 + rel].astype(F32)
    for value, at in ((same, b), (other, 1 - b)):
        value = jnp.log1p(value)
        out[:, pl.ds(pl.multiple_of(at * TRK, TRK), 256)] = value[0:8]
        out[:, pl.ds(pl.multiple_of(at * TRK + 256, 256), 256)] = value[8:16]


def local(feats, conv_w, conv_bias, qkv_w, out_w, head_w, head_bias, exon_lists):
    vmem = pltpu.VMEM
    dma = pltpu.SemaphoreType.DMA
    anywhere = pl.BlockSpec(memory_space=pltpu.HBM)
    return pl.pallas_call(
        kernel,
        out_shape=vmem((8, 1024), F32),
        in_specs=[anywhere] * 8,
        out_specs=pl.BlockSpec(memory_space=pltpu.VMEM),
        scratch_shapes=[
            vmem((D, BINS), BF16),
            vmem((TAPS, ROWS, 2 * COLS), BF16),
            vmem((ROWS, 640), BF16),
            vmem((384,), F32),
            vmem((8, 128), F32),
            vmem((3, 8, 64), jnp.int32),
            vmem((ROWS, WIDE), BF16),
            vmem((ROWS, WIDE2), BF16),
            vmem((ROWS, TAIL), BF16),
            vmem((ROWS, KV), BF16),
            vmem((ROWS, TRK), BF16),
            vmem((ROWS, 2 * COLS), BF16),
            vmem((D, WIDE), BF16),
            vmem((D, WIDE2), BF16),
            vmem((D, TAIL), BF16),
            vmem((D, KV), BF16),
            vmem((D, TRK), BF16),
            vmem((D, D // 2), BF16),
            vmem((D, D // 2), BF16),
            vmem((D, BINS), BF16),
            vmem((D, BINS), BF16),
            vmem((D, BINS), BF16),
            vmem((BINS, D), BF16),
            vmem((BINS, WIDE + WIDE2), F32),
            vmem((128, D), BF16),
            vmem((KV, D), BF16),
            vmem((TRK, D), BF16),
            vmem((TRK, 1), F32),
            vmem((TRK, BINS), BF16),
            vmem((512, BINS), BF16),
            vmem((2, 32, 16, 128), BF16),
            vmem((2, 32, 16, 128), BF16),
            vmem((32, 16, 256), BF16),
            vmem((32, 16, 256), BF16),
            dma((7, 32)), dma((7, 34)), dma((4,)), dma((4,)),
            dma((4, 8)), dma((4, 8)), dma((32,)), dma((32,)), dma((2,)), dma((2,)), dma((20,)),
        ],
        compiler_params=pltpu.CompilerParams(
            collective_id=0, has_side_effects=True, vmem_limit_bytes=60 * 1024 * 1024
        ),
    )(
        feats[0],
        conv_w.transpose(1, 0, 2),
        qkv_w,
        out_w,
        head_w,
        conv_bias,
        head_bias.reshape(8, 128),
        exon_lists[:, 0].transpose(0, 2, 1),
    )


def solution(mesh):
    in_specs = (
        P("win", None, None),
        P("win", None, "mp"),
        P("mp"),
        P("win", "mp"),
        P("win", "mp"),
        P("win", "mp"),
        P("mp"),
        P(None, "win", None, None),
    )
    return jax.shard_map(
        local, mesh=mesh, in_specs=in_specs, out_specs=P(("segment", "win"), "mp"), check_vma=False
    )
```

```python
import math

import jax
import jax.numpy as jnp
from jax import lax
from jax.experimental import pallas as pl
from jax.experimental.pallas import tpu as pltpu
from jax.sharding import PartitionSpec as P

MESH = pl.DeviceIdType.MESH
F32 = jnp.float32
BF16 = jnp.bfloat16

KEY = 64
VAL = 192
TAPS = 5
STEP = 4
BINS = 256
D = 1536
ROWS = 48
COLS = 192
WIDE = 384
WIDE2 = 256
TAIL = 384
KV = 256
TRK = 512
NZ = 8
NY = 4

TREE = {
    ("O", 0): ("zp2", "zm2", "xp"),
    ("X", 0): ("zm",),
    ("O", -2): ("xp", "zm", "zp"),
    ("O", 2): ("zm", "xp", "zp"),
    ("X", 1): (),
    ("X", -2): ("zp2",),
    ("O", -3): ("xp",),
    ("O", -1): ("xp",),
    ("X", 2): ("zm",),
    ("O", 1): (),
    ("O", 3): ("zm",),
    ("X", -3): (),
    ("X", 3): (),
    ("X", -1): (),
    ("O", -4): (),
    ("X", -4): (),
}
EARLY = (
    (0, "O", 0), (1, "O", 0), (2, "O", 0), (0, "X", 0), (1, "X", 0), (2, "X", 0), (0, "O", -2), (0, "O", 2),
    (1, "O", -2), (1, "O", 2), (2, "O", -2), (2, "O", 2), (0, "X", 1), (1, "X", 1), (2, "X", 1), (0, "X", -2),
    (0, "O", -3), (0, "O", -1), (0, "X", 2), (0, "O", 1), (1, "X", -2), (0, "O", 3), (1, "O", -3), (1, "X", 2),
    (1, "O", -1), (1, "O", 1), (1, "O", 3), (2, "X", -2), (2, "O", -3), (2, "O", -1), (2, "X", 2), (2, "O", 1),
    (2, "O", 3), (0, "X", -3), (0, "X", 3), (0, "X", -1), (1, "X", -3), (0, "O", -4), (0, "X", -4), (1, "X", -1),
    (1, "X", 3), (1, "O", -4), (1, "X", -4), (2, "X", -3), (2, "X", 3), (2, "X", -1), (2, "O", -4), (2, "X", -4),
)
LEAN = (
    ((("O", 0), ("zp", "zm", "xp", "cp")),),
    ((("O", -1), ("zp", "cp")), (("O", 1), ("zm", "cp")), (("X", 0), ("zp", "zm", "cp"))),
    (
        (("O", -2), ("zp", "xp", "cp")),
        (("O", 2), ("zm", "cp")),
        (("X", 1), ("zm", "cp")),
        (("X", -1), ("cp",)),
    ),
    (
        (("O", -3), ("zp", "xp", "cp")),
        (("O", 3), ("xp", "cp")),
        (("X", 2), ("cp",)),
        (("X", -2), ("cp",)),
    ),
    ((("O", -4), ("xp", "cp")), (("X", 3), ("cp",)), (("X", -3), ("cp",))),
    ((("X", -4), ("cp",)),),
)


def nt(left, right):
    return lax.dot_general(left, right, (((1,), (1,)), ((), ())), preferred_element_type=F32)


def nn(left, right):
    return lax.dot_general(left, right, (((1,), (0,)), ((), ())), preferred_element_type=F32)


def tn(left, right):
    return lax.dot_general(left, right, (((0,), (0,)), ((), ())), preferred_element_type=F32)


def gelu(x):
    return 0.5 * x * (1.0 + jnp.tanh(math.sqrt(2.0 / math.pi) * (x + 0.044715 * (x * x * x))))


def kernel(
    feats_h, conv_h, qkv_h, outw_h, head_h, cbias_h, hbias_h, exon_h,
    out,
    feats, conv, qkv, cbias, hbias, exon, pa, pa2, pb, pk, ph, po,
    wa, wa2, wb, wk, wh, wo, wo2, gx, ga, gr, ft, y, wqt, wkt, wht, hcol, trk, gmat, ex_out, ex_in, gs, gin,
    ring_r, ring_s, rsy, ssy, rsa, ssa, rsg, ssg, rse, sse, lsem,
):
    s = lax.axis_index("segment")
    w = lax.axis_index("win")
    m = lax.axis_index("mp")
    h = w // (2 * NZ)
    z = (w // 2) % NZ
    c = w % 2
    b = (s + h) % 2
    q = 2 * m + b

    def win_of(hh, zz, cc):
        return hh * (2 * NZ) + zz * 2 + cc

    where = {
        "zp": {"win": win_of(h, (z + 1) % NZ, c)},
        "zm": {"win": win_of(h, (z + NZ - 1) % NZ, c)},
        "zp2": {"win": win_of(h, (z + 2) % NZ, c)},
        "zm2": {"win": win_of(h, (z + NZ - 2) % NZ, c)},
        "xp": {"segment": 1 - s, "win": win_of(1 - h, z, c)},
        "cp": {"win": win_of(h, z, 1 - c)},
        "sp": {"segment": 1 - s},
        "yp": {"mp": (m + 1) % NY},
        "ym": {"mp": (m + NY - 1) % NY},
        "y2": {"mp": (m + 2) % NY},
    }

    def to(name):
        d = {"segment": s, "win": w, "mp": m}
        d.update(where[name])
        return (d["segment"], d["win"], d["mp"])

    barrier = pltpu.get_barrier_semaphore()
    for name in where:
        pl.semaphore_signal(barrier, inc=1, device_id=to(name), device_id_type=MESH)

    local_copies = [
        pltpu.make_async_copy(src, dst, lsem.at[i])
        for i, (src, dst) in enumerate(
            (
                (conv_h, conv),
                (qkv_h, qkv),
                (feats_h, feats),
                (head_h.at[:, pl.ds(pl.multiple_of(b * TRK, TRK), TRK)], ph),
                (outw_h, po),
                (exon_h, exon),
                (cbias_h, cbias),
                (hbias_h, hbias),
            )
        )
    ]
    for copy in local_copies:
        copy.start()

    def remote(src, dst, send, recv, device):
        return pltpu.make_async_remote_copy(
            src_ref=src, dst_ref=dst, send_sem=send, recv_sem=recv, device_id=device, device_id_type=MESH
        )

    lane = lax.broadcasted_iota(jnp.int32, (1, 128), 1)
    low = lane < 64
    local_copies[0].wait()
    local_copies[1].wait()
    thin = []
    for tap in range(TAPS):
        part = conv[tap].astype(F32)
        part = jnp.where(b == 0, part, pltpu.roll(part, COLS, 1))
        if tap < 3:
            pa[:, tap * 128 : tap * 128 + 128] = part[:, :128].astype(BF16)
        else:
            pa2[:, tap * 128 - 384 : tap * 128 - 256] = part[:, :128].astype(BF16)
        thin.append(part[:, 128:256])
    head_part = qkv[...].astype(F32)
    head_part = jnp.where(b == 0, head_part, pltpu.roll(head_part, 320, 1))
    thin.append(head_part[:, :128])
    for i in range(3):
        pb[:, i * 128 : i * 128 + 128] = jnp.where(low, thin[2 * i], pltpu.roll(thin[2 * i + 1], 64, 1)).astype(BF16)
    pk[...] = pltpu.roll(head_part, 576, 1)[:, :KV].astype(BF16)

    pl.semaphore_wait(barrier, len(where))

    def ring(index, plan, own, buf):
        count = [0]
        tail = []

        def rows(win):
            return buf.at[pl.ds(pl.multiple_of(win * ROWS, ROWS), ROWS), :]

        def shard_win(code, core):
            kind, d = code
            return win_of(h if kind == "O" else 1 - h, (z + d + NZ) % NZ, core)

        def recv(win):
            return ring_r.at[index, win]

        def wait(win):
            remote(rows(win), rows(win), ring_s.at[index, 0], recv(win), to("cp")).wait_recv()

        def take(code, names):
            win = shard_win(code, c)
            src = rows(win)
            if code == ("O", 0):
                src = rows(win) if own is None else own
            else:
                wait(win)
            for name in names:
                copy = remote(src, rows(win), ring_s.at[index, count[0]], recv(win), to(name))
                count[0] += 1
                copy.start()
                tail.append(copy)

        def step(r):
            if plan is None:
                take(r, TREE[r] + ("cp",))
            else:
                for code, names in plan[r]:
                    take(code, names)

        def rest():
            for code in TREE:
                wait(shard_win(code, 1 - c))

        def flush():
            for copy in tail:
                copy.wait_send()

        keep = None
        if own is not None:
            keep = pltpu.make_async_copy(own, rows(w), lsem.at[13 + index])
        return step, rest, flush, keep

    def gather(buf, index, lo, n):
        def rows(dm, other, skip=0, count=n):
            slot = 2 * ((m + dm + NY) % NY) + (1 - b if other else b)
            return buf.at[pl.ds(pl.multiple_of(slot * COLS + lo + skip, 16), count), :]

        half = n // 2
        tail = []

        def push(i, ref, name):
            copy = remote(ref, ref, ssa.at[index, i], rsa.at[index, i], to(name))
            copy.start()
            tail.append(copy)

        def got(i, ref):
            remote(ref, ref, ssa.at[index, i], rsa.at[index, i], to("sp")).wait_recv()

        def start():
            own = rows(0, False)
            push(0, own, "yp")
            push(1, own, "ym")
            push(2, own, "sp")

        def first():
            got(0, rows(-1, False))
            push(3, rows(-1, False, 0, half), "yp")
            got(1, rows(1, False))
            push(4, rows(1, False, half, half), "ym")
            got(2, rows(0, True))
            push(5, rows(0, True), "yp")
            push(6, rows(0, True), "ym")

        def second():
            got(3, rows(2, False, 0, half))
            got(4, rows(2, False, half, half))
            push(7, rows(2, False), "sp")

        def third():
            got(5, rows(-1, True))
            got(6, rows(1, True))
            got(7, rows(2, True))

        def flush():
            for copy in tail:
                copy.wait_send()

        return start, first, second, third, flush

    step_a, rest_a, flush_a, keep_a = ring(0, None, pa, wa)
    step_a2, rest_a2, flush_a2, keep_a2 = ring(6, None, pa2, wa2)
    step_b, rest_b, flush_b, keep_b = ring(1, None, pb, wb)
    step_k, rest_k, flush_k, keep_k = ring(2, LEAN, pk, wk)
    step_h, rest_h, flush_h, keep_h = ring(3, LEAN, ph, wh)
    step_o, rest_o, flush_o, _ = ring(4, LEAN, None, wo)
    step_p, rest_p, flush_p, _ = ring(5, LEAN, None, wo2)

    start_x, first_x, second_x, third_x, flush_x = gather(gx, 0, 0, 128)
    start_u, first_u, second_u, third_u, flush_u = gather(gx, 1, 128, 64)
    start_v, first_v, second_v, third_v, flush_v = gather(ga, 2, 0, 96)
    start_w, first_w, second_w, third_w, flush_w = gather(ga, 3, 96, 96)

    early_steps = (step_a, step_a2, step_b)

    def early(first, last):
        for stream, kind, d in EARLY[first:last]:
            early_steps[stream]((kind, d))

    early(0, 3)
    keep_a.start()
    keep_a2.start()
    keep_b.start()
    keep_k.start()

    def wo_part(buf, model):
        return buf.at[
            pl.ds(pl.multiple_of(w * ROWS, ROWS), ROWS),
            pl.ds(pl.multiple_of((model % 2) * 2 * COLS, 2 * COLS), 2 * COLS),
        ]

    for i in range(2, len(local_copies)):
        local_copies[i].wait()
    keep_h.start()

    def each_part(model, act):
        @pl.when(model < 2)
        def _():
            act(wo_part(wo, model))

        @pl.when(model >= 2)
        def _():
            act(wo_part(wo2, model))

    hops = (("yp", 1), ("ym", 3), ("y2", 2))
    each_part(m, lambda ref: pltpu.make_async_copy(po, ref, lsem.at[12]).start())
    for name, j in hops:
        each_part(m, lambda ref, name=name, j=j: remote(po, ref, ssy.at[j], rsy.at[j], to(name)).start())

    def wo_ready():
        each_part(m, lambda ref: pltpu.make_async_copy(po, ref, lsem.at[12]).wait())
        for name, j in hops:
            each_part(
                (m - j + NY) % NY, lambda ref, j=j: remote(po, ref, ssy.at[j], rsy.at[j], to("cp")).wait_recv()
            )

    eye = (
        lax.broadcasted_iota(jnp.int32, (BINS, BINS), 0) == lax.broadcasted_iota(jnp.int32, (BINS, BINS), 1)
    ).astype(F32).astype(BF16)

    early(3, 9)

    rows_id = lax.broadcasted_iota(jnp.int32, (512, 64), 0)
    owner = (
        ((rows_id // 128) % 2) * 32 + ((rows_id // 64) % 2) * 16 + ((rows_id // 8) % 8) * 2 + rows_id // 256
    )
    repeat = (owner == lax.broadcasted_iota(jnp.int32, (512, 64), 1)).astype(F32).astype(BF16)
    first_bin = nt(repeat, exon[0].astype(F32).astype(BF16))
    end_bin = nt(repeat, exon[1].astype(F32).astype(BF16))
    gene = nt(repeat, exon[2].astype(F32).astype(BF16))

    def gene_bins(blk):
        at = slice(blk * 64, blk * 64 + 64)
        bins = lax.broadcasted_iota(jnp.int32, (64, BINS), 1).astype(F32)
        which = (lax.broadcasted_iota(jnp.int32, (64, 1), 0) % 8).astype(F32)
        total = jnp.zeros((64, BINS), F32)
        for j in range(8):
            lo = jnp.where(gene[at, j : j + 1] == which, first_bin[at, j : j + 1], 1024.0)
            inside = jnp.logical_and(bins >= lo, bins < end_bin[at, j : j + 1])
            total = total + jnp.where(inside, 1.0, 0.0)
        gmat[at, :] = total.astype(BF16)

    gene_bins(0)
    early(9, 14)
    step_k(0)
    early(14, 17)
    gene_bins(1)
    early(17, 25)
    step_h(0)
    @pl.loop(0, D // BINS)
    def _(n):
        at = pl.ds(pl.multiple_of(n * BINS, BINS), BINS)
        ft[:, at] = nt(eye, feats[at, :]).astype(BF16)

    early(25, 31)
    step_k(1)
    early(31, 39)
    step_h(1)
    wo_ready()
    early(39, 43)
    step_o(0)
    step_p(0)
    step_k(2)
    early(43, 48)
    keep_a.wait()
    keep_a2.wait()
    rest_a()
    rest_a2()

    t_row = lax.broadcasted_iota(jnp.int32, (BINS, 128), 0)

    def shifted(x, tap):
        by = (tap - TAPS // 2) * STEP
        if by == 0:
            return x
        moved = pltpu.roll(x, (BINS - by) % BINS, 0)
        ok = jnp.logical_and(t_row + by >= 0, t_row + by < BINS)
        return jnp.where(ok, moved, 0.0)

    c0, c1, c2 = (cbias[i * 128 : i * 128 + 128].reshape(1, 128) for i in range(3))
    wide_bias = jnp.where(b == 0, c0, pltpu.roll(jnp.where(low, c2, c1), 64, 1))
    narrow_bias = jnp.where(b == 0, c1, pltpu.roll(c2, 64, 1))
    base = pl.multiple_of(q * COLS, COLS)
    base2 = pl.multiple_of(q * COLS + 128, 64)

    for i in range(TAPS):
        part = wa[:, i * 128 : i * 128 + 128] if i < 3 else wa2[:, i * 128 - 384 : i * 128 - 256]
        y[:, i * 128 : i * 128 + 128] = nn(ft[...], part)
    wide = shifted(y[:, 0:128], 0)
    for tap in range(1, TAPS):
        wide = wide + shifted(y[:, tap * 128 : tap * 128 + 128], tap)
    wide = gelu(wide + wide_bias).T
    gx[pl.ds(base, 128), :] = (feats[pl.ds(base, 128), :].astype(F32) + wide).astype(BF16)
    start_x()

    keep_b.wait()
    rest_b()
    step_o(1)
    pairs = [nn(ft[...], wb[:, i * 128 : i * 128 + 128]) for i in range(3)]
    even = shifted(pairs[0], 0) + shifted(pairs[1], 2) + shifted(pairs[2], 4)
    odd = shifted(pairs[0], 1) + shifted(pairs[1], 3)
    narrow = even + pltpu.roll(odd, 64, 1)
    narrow = gelu(narrow + narrow_bias).T
    gx[pl.ds(base2, 64), :] = (feats[pl.ds(base2, 64), :].astype(F32) + narrow[:64]).astype(BF16)
    start_u()
    step_h(2)
    step_k(3)
    step_p(1)
    first_x()
    for blk in range(2, 4):
        gene_bins(blk)
    first_u()
    step_o(2)
    wqt[...] = nt(eye[:128, :128], wb[:, 256:384]).astype(BF16)
    second_x()
    step_k(4)
    step_h(3)
    second_u()
    step_p(2)
    third_x()
    step_k(5)
    third_u()
    keep_k.wait()
    rest_k()
    wkt[...] = nt(eye, wk[...]).astype(BF16)

    qq = nn(wqt[...], gx[...])[64:128].astype(BF16)
    kv = nn(wkt[...], gx[...]).astype(BF16)
    scores = tn(kv[0:64], qq) * (1.0 / math.sqrt(KEY))
    weights = jnp.exp(scores)
    prob = (weights / jnp.sum(weights, axis=0, keepdims=True)).astype(BF16)
    ga[pl.ds(base, COLS), :] = nn(kv[64:256], prob).astype(BF16)

    start_v()
    start_w()
    step_o(3)
    step_h(4)
    step_p(3)
    for blk in range(4, 6):
        gene_bins(blk)
    first_v()
    step_h(5)
    step_o(4)
    first_w()
    keep_h.wait()
    rest_h()
    for blk in range(6, 8):
        gene_bins(blk)
    step_p(4)
    second_v()
    step_o(5)
    second_w()
    for i in range(TRK // 256):
        wht[i * 256 : i * 256 + 256, :] = nt(eye, wh[:, i * 256 : i * 256 + 256]).astype(BF16)
    eye_f = (
        lax.broadcasted_iota(jnp.int32, (128, 128), 0) == lax.broadcasted_iota(jnp.int32, (128, 128), 1)
    )
    for i in range(TRK // 128):
        row = jnp.where(b == 0, hbias[i : i + 1, :], hbias[4 + i : 5 + i, :])
        hcol[i * 128 : i * 128 + 128, :] = jnp.sum(jnp.where(eye_f, row, 0.0), axis=1, keepdims=True)
    step_p(5)
    flush_a()
    flush_a2()
    flush_b()
    third_v()
    third_w()
    rest_o()
    rest_p()

    for i in range(D // 256):
        at = slice(i * 256, i * 256 + 256)
        gr[at, :] = (gx[at, :].astype(F32) + (nn(wo[at, :], ga[0 : D // 2, :]) + nn(wo2[at, :], ga[D // 2 :, :]))).astype(BF16)

    def sums(core, blk):
        rows = gmat[pl.ds(pl.multiple_of(core * 256, 256), 256), :]
        return nt(rows, trk[blk * 256 : blk * 256 + 256, :]).reshape(32, 8, 256)

    swaps = []
    for blk in range(TRK // 256):
        at = slice(blk * 256, blk * 256 + 256)
        logits = nn(wht[at, :], gr[...]) + hcol[at, :]
        soft = jnp.maximum(logits, 0.0) + jnp.log1p(jnp.exp(-jnp.abs(logits)))
        trk[at, :] = soft.astype(BF16)
        give = sums(1 - c, blk)
        ex_out[blk] = jnp.concatenate([give[:, :, :128], give[:, :, 128:]], axis=1).astype(BF16)
        swaps.append(remote(ex_out.at[blk], ex_in.at[blk], sse.at[blk], rse.at[blk], to("cp")))
        swaps[blk].start()
    keep_sums = [sums(c, blk) for blk in range(TRK // 256)]
    for blk in range(TRK // 256):
        swaps[blk].wait_recv()
        took = ex_in[blk].astype(F32)
        keep_sums[blk] = keep_sums[blk] + jnp.concatenate([took[:, :8], took[:, 8:]], axis=2)
    gs[...] = jnp.concatenate(keep_sums, axis=1).astype(BF16)

    def gene_copy(rel):
        ds, dh, dz = rel // 16, (rel // 8) % 2, rel % 8
        s2, h2, z2 = (s + ds) % 2, (h + dh) % 2, (z + dz) % NZ
        return remote(
            gs.at[s2 * 16 + h2 * 8 + z2],
            gin.at[rel],
            ssg.at[rel],
            rsg.at[rel],
            (s2, win_of(h2, z2, c), m),
        )

    gene_copies = [gene_copy(part * 8 + dz) for dz in (4, 3, 5, 2, 6, 1, 7, 0) for part in (3, 2, 1, 0) if part + dz]
    for copy in gene_copies:
        copy.start()

    gin[0] = gs[s * 16 + h * 8 + z]
    flush_k()
    flush_h()
    flush_o()
    flush_p()
    flush_x()
    flush_u()
    flush_v()
    flush_w()
    for name, j in hops:
        each_part(m, lambda ref, name=name, j=j: remote(po, ref, ssy.at[j], rsy.at[j], to(name)).wait_send())
    for swap in swaps:
        swap.wait_send()
    for copy in gene_copies:
        copy.wait()

    same = gin[0].astype(F32)
    other = gin[8].astype(F32)
    for rel in range(1, 8):
        same = same + gin[rel].astype(F32)
        other = other + gin[8 + rel].astype(F32)
    for rel in range(8):
        other = other + gin[16 + rel].astype(F32)
        same = same + gin[24 + rel].astype(F32)
    for value, at in ((same, b), (other, 1 - b)):
        value = jnp.log1p(value)
        out[:, pl.ds(pl.multiple_of(at * TRK, TRK), 256)] = value[0:8]
        out[:, pl.ds(pl.multiple_of(at * TRK + 256, 256), 256)] = value[8:16]


def local(feats, conv_w, conv_bias, qkv_w, out_w, head_w, head_bias, exon_lists):
    vmem = pltpu.VMEM
    dma = pltpu.SemaphoreType.DMA
    anywhere = pl.BlockSpec(memory_space=pltpu.HBM)
    return pl.pallas_call(
        kernel,
        out_shape=vmem((8, 1024), F32),
        in_specs=[anywhere] * 8,
        out_specs=pl.BlockSpec(memory_space=pltpu.VMEM),
        scratch_shapes=[
            vmem((D, BINS), BF16),
            vmem((TAPS, ROWS, 2 * COLS), BF16),
            vmem((ROWS, 640), BF16),
            vmem((384,), F32),
            vmem((8, 128), F32),
            vmem((3, 8, 64), jnp.int32),
            vmem((ROWS, WIDE), BF16),
            vmem((ROWS, WIDE2), BF16),
            vmem((ROWS, TAIL), BF16),
            vmem((ROWS, KV), BF16),
            vmem((ROWS, TRK), BF16),
            vmem((ROWS, 2 * COLS), BF16),
            vmem((D, WIDE), BF16),
            vmem((D, WIDE2), BF16),
            vmem((D, TAIL), BF16),
            vmem((D, KV), BF16),
            vmem((D, TRK), BF16),
            vmem((D, D // 2), BF16),
            vmem((D, D // 2), BF16),
            vmem((D, BINS), BF16),
            vmem((D, BINS), BF16),
            vmem((D, BINS), BF16),
            vmem((BINS, D), BF16),
            vmem((BINS, WIDE + WIDE2), F32),
            vmem((128, D), BF16),
            vmem((KV, D), BF16),
            vmem((TRK, D), BF16),
            vmem((TRK, 1), F32),
            vmem((TRK, BINS), BF16),
            vmem((512, BINS), BF16),
            vmem((2, 32, 16, 128), BF16),
            vmem((2, 32, 16, 128), BF16),
            vmem((32, 16, 256), BF16),
            vmem((32, 16, 256), BF16),
            dma((7, 32)), dma((7, 34)), dma((4,)), dma((4,)),
            dma((4, 8)), dma((4, 8)), dma((32,)), dma((32,)), dma((2,)), dma((2,)), dma((20,)),
        ],
        compiler_params=pltpu.CompilerParams(
            collective_id=0, has_side_effects=True, vmem_limit_bytes=60 * 1024 * 1024
        ),
    )(
        feats[0],
        conv_w.transpose(1, 0, 2),
        qkv_w,
        out_w,
        head_w,
        conv_bias,
        head_bias.reshape(8, 128),
        exon_lists[:, 0].transpose(0, 2, 1),
    )


def solution(mesh):
    in_specs = (
        P("win", None, None),
        P("win", None, "mp"),
        P("mp"),
        P("win", "mp"),
        P("win", "mp"),
        P("win", "mp"),
        P("mp"),
        P(None, "win", None, None),
    )
    return jax.shard_map(
        local, mesh=mesh, in_specs=in_specs, out_specs=P(("segment", "win"), "mp"), check_vma=False
    )
```

```python
import math

import jax
import jax.numpy as jnp
from jax import lax
from jax.experimental import pallas as pl
from jax.experimental.pallas import tpu as pltpu
from jax.sharding import PartitionSpec as P

MESH = pl.DeviceIdType.MESH
F32 = jnp.float32
BF16 = jnp.bfloat16

KEY = 64
VAL = 192
TAPS = 5
STEP = 4
BINS = 256
D = 1536
ROWS = 48
COLS = 192
WIDE = 640
TAIL = 384
KV = 256
TRK = 512
NZ = 8
NY = 4

QUICK = (
    ((("O", 0), ("zp", "zm", "xp", "zp2", "zm2", "cp")),),
    (
        (("O", -1), ("cp",)),
        (("O", 1), ("cp",)),
        (("X", 0), ("zp", "zm", "cp")),
        (("O", -2), ("zp", "xp", "cp")),
        (("O", 2), ("zm", "cp")),
    ),
    (
        (("O", -3), ("zp", "xp", "cp")),
        (("O", 3), ("xp", "cp")),
        (("X", 1), ("zm", "cp")),
        (("X", -1), ("cp",)),
        (("X", -2), ("cp",)),
    ),
    (
        (("O", -4), ("xp", "cp")),
        (("X", 2), ("cp",)),
        (("X", 3), ("cp",)),
        (("X", -3), ("cp",)),
    ),
    ((("X", -4), ("cp",)),),
)
LEAN = (
    ((("O", 0), ("zp", "zm", "xp", "cp")),),
    ((("O", -1), ("zp", "cp")), (("O", 1), ("zm", "cp")), (("X", 0), ("zp", "zm", "cp"))),
    (
        (("O", -2), ("zp", "xp", "cp")),
        (("O", 2), ("zm", "cp")),
        (("X", 1), ("zm", "cp")),
        (("X", -1), ("cp",)),
    ),
    (
        (("O", -3), ("zp", "xp", "cp")),
        (("O", 3), ("xp", "cp")),
        (("X", 2), ("cp",)),
        (("X", -2), ("cp",)),
    ),
    ((("O", -4), ("xp", "cp")), (("X", 3), ("cp",)), (("X", -3), ("cp",))),
    ((("X", -4), ("cp",)),),
)


def nt(left, right):
    return lax.dot_general(left, right, (((1,), (1,)), ((), ())), preferred_element_type=F32)


def nn(left, right):
    return lax.dot_general(left, right, (((1,), (0,)), ((), ())), preferred_element_type=F32)


def tn(left, right):
    return lax.dot_general(left, right, (((0,), (0,)), ((), ())), preferred_element_type=F32)


def gelu(x):
    return 0.5 * x * (1.0 + jnp.tanh(math.sqrt(2.0 / math.pi) * (x + 0.044715 * (x * x * x))))


def kernel(
    feats_h, conv_h, qkv_h, outw_h, head_h, cbias_h, hbias_h, exon_h,
    out,
    feats, conv, qkv, cbias, hbias, exon, pa, pb, pk, ph, po,
    wa, wb, wk, wh, wo, wo2, gx, ga, gr, ft, y, wqt, wkt, wht, hcol, trk, gmat, ex_out, ex_in, gs, gin,
    ring_r, ring_s, rsy, ssy, rsa, ssa, rsg, ssg, rse, sse, lsem,
):
    s = lax.axis_index("segment")
    w = lax.axis_index("win")
    m = lax.axis_index("mp")
    h = w // (2 * NZ)
    z = (w // 2) % NZ
    c = w % 2
    b = (s + h) % 2
    q = 2 * m + b

    def win_of(hh, zz, cc):
        return hh * (2 * NZ) + zz * 2 + cc

    where = {
        "zp": {"win": win_of(h, (z + 1) % NZ, c)},
        "zm": {"win": win_of(h, (z + NZ - 1) % NZ, c)},
        "zp2": {"win": win_of(h, (z + 2) % NZ, c)},
        "zm2": {"win": win_of(h, (z + NZ - 2) % NZ, c)},
        "xp": {"segment": 1 - s, "win": win_of(1 - h, z, c)},
        "cp": {"win": win_of(h, z, 1 - c)},
        "sp": {"segment": 1 - s},
        "yp": {"mp": (m + 1) % NY},
        "ym": {"mp": (m + NY - 1) % NY},
        "y2": {"mp": (m + 2) % NY},
    }

    def to(name):
        d = {"segment": s, "win": w, "mp": m}
        d.update(where[name])
        return (d["segment"], d["win"], d["mp"])

    barrier = pltpu.get_barrier_semaphore()
    for name in where:
        pl.semaphore_signal(barrier, inc=1, device_id=to(name), device_id_type=MESH)

    local_copies = [
        pltpu.make_async_copy(src, dst, lsem.at[i])
        for i, (src, dst) in enumerate(
            (
                (conv_h, conv),
                (qkv_h, qkv),
                (feats_h, feats),
                (head_h.at[:, pl.ds(pl.multiple_of(b * TRK, TRK), TRK)], ph),
                (outw_h, po),
                (exon_h, exon),
                (cbias_h, cbias),
                (hbias_h, hbias),
            )
        )
    ]
    for copy in local_copies:
        copy.start()

    def remote(src, dst, send, recv, device):
        return pltpu.make_async_remote_copy(
            src_ref=src, dst_ref=dst, send_sem=send, recv_sem=recv, device_id=device, device_id_type=MESH
        )

    lane = lax.broadcasted_iota(jnp.int32, (1, 128), 1)
    low = lane < 64
    local_copies[0].wait()
    local_copies[1].wait()
    thin = []
    for tap in range(TAPS):
        part = conv[tap].astype(F32)
        part = jnp.where(b == 0, part, pltpu.roll(part, COLS, 1))
        pa[:, tap * 128 : tap * 128 + 128] = part[:, :128].astype(BF16)
        thin.append(part[:, 128:256])
    head_part = qkv[...].astype(F32)
    head_part = jnp.where(b == 0, head_part, pltpu.roll(head_part, 320, 1))
    thin.append(head_part[:, :128])
    for i in range(3):
        pb[:, i * 128 : i * 128 + 128] = jnp.where(low, thin[2 * i], pltpu.roll(thin[2 * i + 1], 64, 1)).astype(BF16)
    pk[...] = pltpu.roll(head_part, 576, 1)[:, :KV].astype(BF16)

    pl.semaphore_wait(barrier, len(where))

    def ring(index, plan, own, buf):
        count = [0]
        tail = []

        def rows(win):
            return buf.at[pl.ds(pl.multiple_of(win * ROWS, ROWS), ROWS), :]

        def shard_win(code, core):
            kind, d = code
            return win_of(h if kind == "O" else 1 - h, (z + d + NZ) % NZ, core)

        def recv(win):
            return ring_r.at[index, win]

        def wait(win):
            remote(rows(win), rows(win), ring_s.at[index, 0], recv(win), to("cp")).wait_recv()

        def step(r):
            for code, names in plan[r]:
                win = shard_win(code, c)
                src = rows(win)
                if code == ("O", 0):
                    src = rows(win) if own is None else own
                else:
                    wait(win)
                for name in names:
                    copy = remote(src, rows(win), ring_s.at[index, count[0]], recv(win), to(name))
                    count[0] += 1
                    copy.start()
                    tail.append(copy)

        def rest():
            for group in plan:
                for code, names in group:
                    wait(shard_win(code, 1 - c))

        def flush():
            for copy in tail:
                copy.wait_send()

        keep = None
        if own is not None:
            keep = pltpu.make_async_copy(own, rows(w), lsem.at[8 + index])
        return step, rest, flush, keep

    def gather(buf, index, lo, n):
        def rows(dm, other, skip=0, count=n):
            slot = 2 * ((m + dm + NY) % NY) + (1 - b if other else b)
            return buf.at[pl.ds(pl.multiple_of(slot * COLS + lo + skip, 16), count), :]

        half = n // 2
        tail = []

        def push(i, ref, name):
            copy = remote(ref, ref, ssa.at[index, i], rsa.at[index, i], to(name))
            copy.start()
            tail.append(copy)

        def got(i, ref):
            remote(ref, ref, ssa.at[index, i], rsa.at[index, i], to("sp")).wait_recv()

        def start():
            own = rows(0, False)
            push(0, own, "yp")
            push(1, own, "ym")
            push(2, own, "sp")

        def first():
            got(0, rows(-1, False))
            push(3, rows(-1, False, 0, half), "yp")
            got(1, rows(1, False))
            push(4, rows(1, False, half, half), "ym")
            got(2, rows(0, True))
            push(5, rows(0, True), "yp")
            push(6, rows(0, True), "ym")

        def second():
            got(3, rows(2, False, 0, half))
            got(4, rows(2, False, half, half))
            push(7, rows(2, False), "sp")

        def third():
            got(5, rows(-1, True))
            got(6, rows(1, True))
            got(7, rows(2, True))

        def flush():
            for copy in tail:
                copy.wait_send()

        return start, first, second, third, flush

    step_a, rest_a, flush_a, keep_a = ring(0, QUICK, pa, wa)
    step_b, rest_b, flush_b, keep_b = ring(1, QUICK, pb, wb)
    step_k, rest_k, flush_k, keep_k = ring(2, LEAN, pk, wk)
    step_h, rest_h, flush_h, keep_h = ring(3, LEAN, ph, wh)
    step_o, rest_o, flush_o, _ = ring(4, LEAN, None, wo)
    step_p, rest_p, flush_p, _ = ring(5, LEAN, None, wo2)

    start_x, first_x, second_x, third_x, flush_x = gather(gx, 0, 0, 128)
    start_u, first_u, second_u, third_u, flush_u = gather(gx, 1, 128, 64)
    start_v, first_v, second_v, third_v, flush_v = gather(ga, 2, 0, 96)
    start_w, first_w, second_w, third_w, flush_w = gather(ga, 3, 96, 96)

    step_a(0)
    step_b(0)
    step_k(0)
    keep_a.start()
    keep_b.start()
    keep_k.start()

    def wo_part(buf, model):
        return buf.at[
            pl.ds(pl.multiple_of(w * ROWS, ROWS), ROWS),
            pl.ds(pl.multiple_of((model % 2) * 2 * COLS, 2 * COLS), 2 * COLS),
        ]

    for i in range(2, len(local_copies)):
        local_copies[i].wait()
    keep_h.start()

    def each_part(model, act):
        @pl.when(model < 2)
        def _():
            act(wo_part(wo, model))

        @pl.when(model >= 2)
        def _():
            act(wo_part(wo2, model))

    hops = (("yp", 1), ("ym", 3), ("y2", 2))
    each_part(m, lambda ref: pltpu.make_async_copy(po, ref, lsem.at[12]).start())
    for name, j in hops:
        each_part(m, lambda ref, name=name, j=j: remote(po, ref, ssy.at[j], rsy.at[j], to(name)).start())

    def wo_ready():
        each_part(m, lambda ref: pltpu.make_async_copy(po, ref, lsem.at[12]).wait())
        for name, j in hops:
            each_part(
                (m - j + NY) % NY, lambda ref, j=j: remote(po, ref, ssy.at[j], rsy.at[j], to("cp")).wait_recv()
            )

    eye = (
        lax.broadcasted_iota(jnp.int32, (BINS, BINS), 0) == lax.broadcasted_iota(jnp.int32, (BINS, BINS), 1)
    ).astype(F32).astype(BF16)

    @pl.loop(0, D // BINS)
    def _(n):
        at = pl.ds(pl.multiple_of(n * BINS, BINS), BINS)
        ft[:, at] = nt(eye, feats[at, :]).astype(BF16)

    step_a(1)
    step_b(1)
    step_h(0)

    rows_id = lax.broadcasted_iota(jnp.int32, (512, 64), 0)
    owner = (
        ((rows_id // 128) % 2) * 32 + ((rows_id // 64) % 2) * 16 + ((rows_id // 8) % 8) * 2 + rows_id // 256
    )
    repeat = (owner == lax.broadcasted_iota(jnp.int32, (512, 64), 1)).astype(F32).astype(BF16)
    first_bin = nt(repeat, exon[0].astype(F32).astype(BF16))
    end_bin = nt(repeat, exon[1].astype(F32).astype(BF16))
    gene = nt(repeat, exon[2].astype(F32).astype(BF16))

    def gene_bins(blk):
        at = slice(blk * 64, blk * 64 + 64)
        bins = lax.broadcasted_iota(jnp.int32, (64, BINS), 1).astype(F32)
        which = (lax.broadcasted_iota(jnp.int32, (64, 1), 0) % 8).astype(F32)
        total = jnp.zeros((64, BINS), F32)
        for j in range(8):
            lo = jnp.where(gene[at, j : j + 1] == which, first_bin[at, j : j + 1], 1024.0)
            inside = jnp.logical_and(bins >= lo, bins < end_bin[at, j : j + 1])
            total = total + jnp.where(inside, 1.0, 0.0)
        gmat[at, :] = total.astype(BF16)

    for blk in range(2):
        gene_bins(blk)
    step_a(2)
    step_b(2)
    step_k(1)
    step_h(1)
    step_a(3)
    step_b(3)
    step_k(2)
    wo_ready()
    step_o(0)
    step_p(0)
    step_a(4)
    step_h(2)
    step_b(4)
    keep_a.wait()
    rest_a()

    t_row = lax.broadcasted_iota(jnp.int32, (BINS, 128), 0)

    def shifted(x, tap):
        by = (tap - TAPS // 2) * STEP
        if by == 0:
            return x
        moved = pltpu.roll(x, (BINS - by) % BINS, 0)
        ok = jnp.logical_and(t_row + by >= 0, t_row + by < BINS)
        return jnp.where(ok, moved, 0.0)

    c0, c1, c2 = (cbias[i * 128 : i * 128 + 128].reshape(1, 128) for i in range(3))
    wide_bias = jnp.where(b == 0, c0, pltpu.roll(jnp.where(low, c2, c1), 64, 1))
    narrow_bias = jnp.where(b == 0, c1, pltpu.roll(c2, 64, 1))
    base = pl.multiple_of(q * COLS, COLS)
    base2 = pl.multiple_of(q * COLS + 128, 64)

    for i in range(TAPS):
        y[:, i * 128 : i * 128 + 128] = nn(ft[...], wa[:, i * 128 : i * 128 + 128])
    wide = shifted(y[:, 0:128], 0)
    for tap in range(1, TAPS):
        wide = wide + shifted(y[:, tap * 128 : tap * 128 + 128], tap)
    wide = gelu(wide + wide_bias).T
    gx[pl.ds(base, 128), :] = (feats[pl.ds(base, 128), :].astype(F32) + wide).astype(BF16)
    start_x()

    keep_b.wait()
    rest_b()
    step_o(1)
    pairs = [nn(ft[...], wb[:, i * 128 : i * 128 + 128]) for i in range(3)]
    even = shifted(pairs[0], 0) + shifted(pairs[1], 2) + shifted(pairs[2], 4)
    odd = shifted(pairs[0], 1) + shifted(pairs[1], 3)
    narrow = even + pltpu.roll(odd, 64, 1)
    narrow = gelu(narrow + narrow_bias).T
    gx[pl.ds(base2, 64), :] = (feats[pl.ds(base2, 64), :].astype(F32) + narrow[:64]).astype(BF16)
    start_u()
    step_k(3)
    step_p(1)
    first_x()
    step_h(3)
    for blk in range(2, 4):
        gene_bins(blk)
    first_u()
    step_o(2)
    wqt[...] = nt(eye[:128, :128], wb[:, 256:384]).astype(BF16)
    second_x()
    step_k(4)
    second_u()
    step_p(2)
    third_x()
    step_k(5)
    step_o(3)
    third_u()
    keep_k.wait()
    rest_k()
    wkt[...] = nt(eye, wk[...]).astype(BF16)

    qq = nn(wqt[...], gx[...])[64:128].astype(BF16)
    kv = nn(wkt[...], gx[...]).astype(BF16)
    scores = tn(kv[0:64], qq) * (1.0 / math.sqrt(KEY))
    weights = jnp.exp(scores)
    prob = (weights / jnp.sum(weights, axis=0, keepdims=True)).astype(BF16)
    ga[pl.ds(base, COLS), :] = nn(kv[64:256], prob).astype(BF16)

    start_v()
    step_h(4)
    step_p(3)
    start_w()
    for blk in range(4, 6):
        gene_bins(blk)
    first_v()
    step_h(5)
    step_o(4)
    first_w()
    keep_h.wait()
    rest_h()
    step_p(4)
    for blk in range(6, 8):
        gene_bins(blk)
    second_v()
    step_o(5)
    second_w()
    for i in range(TRK // 256):
        wht[i * 256 : i * 256 + 256, :] = nt(eye, wh[:, i * 256 : i * 256 + 256]).astype(BF16)
    eye_f = (
        lax.broadcasted_iota(jnp.int32, (128, 128), 0) == lax.broadcasted_iota(jnp.int32, (128, 128), 1)
    )
    for i in range(TRK // 128):
        row = jnp.where(b == 0, hbias[i : i + 1, :], hbias[4 + i : 5 + i, :])
        hcol[i * 128 : i * 128 + 128, :] = jnp.sum(jnp.where(eye_f, row, 0.0), axis=1, keepdims=True)
    step_p(5)
    flush_a()
    flush_b()
    third_v()
    third_w()
    rest_o()
    rest_p()

    for i in range(D // 256):
        at = slice(i * 256, i * 256 + 256)
        gr[at, :] = (gx[at, :].astype(F32) + (nn(wo[at, :], ga[0 : D // 2, :]) + nn(wo2[at, :], ga[D // 2 :, :]))).astype(BF16)

    def sums(core, blk):
        rows = gmat[pl.ds(pl.multiple_of(core * 256, 256), 256), :]
        return nt(rows, trk[blk * 256 : blk * 256 + 256, :]).reshape(32, 8, 256)

    swaps = []
    for blk in range(TRK // 256):
        at = slice(blk * 256, blk * 256 + 256)
        logits = nn(wht[at, :], gr[...]) + hcol[at, :]
        soft = jnp.maximum(logits, 0.0) + jnp.log1p(jnp.exp(-jnp.abs(logits)))
        trk[at, :] = soft.astype(BF16)
        give = sums(1 - c, blk)
        ex_out[blk] = jnp.concatenate([give[:, :, :128], give[:, :, 128:]], axis=1).astype(BF16)
        swaps.append(remote(ex_out.at[blk], ex_in.at[blk], sse.at[blk], rse.at[blk], to("cp")))
        swaps[blk].start()
    keep_sums = [sums(c, blk) for blk in range(TRK // 256)]
    for blk in range(TRK // 256):
        swaps[blk].wait_recv()
        took = ex_in[blk].astype(F32)
        keep_sums[blk] = keep_sums[blk] + jnp.concatenate([took[:, :8], took[:, 8:]], axis=2)
    gs[...] = jnp.concatenate(keep_sums, axis=1).astype(BF16)

    def gene_copy(rel):
        ds, dh, dz = rel // 16, (rel // 8) % 2, rel % 8
        s2, h2, z2 = (s + ds) % 2, (h + dh) % 2, (z + dz) % NZ
        return remote(
            gs.at[s2 * 16 + h2 * 8 + z2],
            gin.at[rel],
            ssg.at[rel],
            rsg.at[rel],
            (s2, win_of(h2, z2, c), m),
        )

    gene_copies = [gene_copy(part * 8 + dz) for dz in (4, 3, 5, 2, 6, 1, 7, 0) for part in (3, 2, 1, 0) if part + dz]
    for copy in gene_copies:
        copy.start()

    gin[0] = gs[s * 16 + h * 8 + z]
    flush_k()
    flush_h()
    flush_o()
    flush_p()
    flush_x()
    flush_u()
    flush_v()
    flush_w()
    for name, j in hops:
        each_part(m, lambda ref, name=name, j=j: remote(po, ref, ssy.at[j], rsy.at[j], to(name)).wait_send())
    for swap in swaps:
        swap.wait_send()
    for copy in gene_copies:
        copy.wait()

    same = gin[0].astype(F32)
    other = gin[8].astype(F32)
    for rel in range(1, 8):
        same = same + gin[rel].astype(F32)
        other = other + gin[8 + rel].astype(F32)
    for rel in range(8):
        other = other + gin[16 + rel].astype(F32)
        same = same + gin[24 + rel].astype(F32)
    for value, at in ((same, b), (other, 1 - b)):
        value = jnp.log1p(value)
        out[:, pl.ds(pl.multiple_of(at * TRK, TRK), 256)] = value[0:8]
        out[:, pl.ds(pl.multiple_of(at * TRK + 256, 256), 256)] = value[8:16]


def local(feats, conv_w, conv_bias, qkv_w, out_w, head_w, head_bias, exon_lists):
    vmem = pltpu.VMEM
    dma = pltpu.SemaphoreType.DMA
    anywhere = pl.BlockSpec(memory_space=pltpu.HBM)
    return pl.pallas_call(
        kernel,
        out_shape=vmem((8, 1024), F32),
        in_specs=[anywhere] * 8,
        out_specs=pl.BlockSpec(memory_space=pltpu.VMEM),
        scratch_shapes=[
            vmem((D, BINS), BF16),
            vmem((TAPS, ROWS, 2 * COLS), BF16),
            vmem((ROWS, 640), BF16),
            vmem((384,), F32),
            vmem((8, 128), F32),
            vmem((3, 8, 64), jnp.int32),
            vmem((ROWS, WIDE), BF16),
            vmem((ROWS, TAIL), BF16),
            vmem((ROWS, KV), BF16),
            vmem((ROWS, TRK), BF16),
            vmem((ROWS, 2 * COLS), BF16),
            vmem((D, WIDE), BF16),
            vmem((D, TAIL), BF16),
            vmem((D, KV), BF16),
            vmem((D, TRK), BF16),
            vmem((D, D // 2), BF16),
            vmem((D, D // 2), BF16),
            vmem((D, BINS), BF16),
            vmem((D, BINS), BF16),
            vmem((D, BINS), BF16),
            vmem((BINS, D), BF16),
            vmem((BINS, WIDE), F32),
            vmem((128, D), BF16),
            vmem((KV, D), BF16),
            vmem((TRK, D), BF16),
            vmem((TRK, 1), F32),
            vmem((TRK, BINS), BF16),
            vmem((512, BINS), BF16),
            vmem((2, 32, 16, 128), BF16),
            vmem((2, 32, 16, 128), BF16),
            vmem((32, 16, 256), BF16),
            vmem((32, 16, 256), BF16),
            dma((6, 32)), dma((6, 34)), dma((4,)), dma((4,)),
            dma((4, 8)), dma((4, 8)), dma((32,)), dma((32,)), dma((2,)), dma((2,)), dma((13,)),
        ],
        compiler_params=pltpu.CompilerParams(
            collective_id=0, has_side_effects=True, vmem_limit_bytes=60 * 1024 * 1024
        ),
    )(
        feats[0],
        conv_w.transpose(1, 0, 2),
        qkv_w,
        out_w,
        head_w,
        conv_bias,
        head_bias.reshape(8, 128),
        exon_lists[:, 0].transpose(0, 2, 1),
    )


def solution(mesh):
    in_specs = (
        P("win", None, None),
        P("win", None, "mp"),
        P("mp"),
        P("win", "mp"),
        P("win", "mp"),
        P("win", "mp"),
        P("mp"),
        P(None, "win", None, None),
    )
    return jax.shard_map(
        local, mesh=mesh, in_specs=in_specs, out_specs=P(("segment", "win"), "mp"), check_vma=False
    )
```
